512 devices in a mesh: shard: 16 (over z), dp: 32 (over x, y, core).
Axes of the slice: x: 4, y: 4, z: 16, core: 2. Of those that a mesh axis runs over, the one named last changes fastest.
Arguments:
- cache_state: float32 [32, 16, 256, 384], P('dp', 'shard'), as said below
- table_state: float32 [32, 16, 512, 384], P('dp', 'shard'), as said below
- batch_idx: int32 [32, 16, 1024, 8], P('dp', 'shard'), may hold values from 0 to 255
- loss_grad: float32 [32, 16, 1024], P('dp', 'shard'), may hold values from -6 to 6
- w_first: bfloat16 [1024, 1024], replicated, may hold values from -0.1875 to 0.1875
- head: float32 [1024], replicated, may hold values from -6 to 6
- home: int32 [32, 8192], P('dp'), may hold values from 0 to 8191, as said below
- fetch_rows: int32 [32, 16, 16, 16], P('dp', 'shard'), may hold values from 0 to 8191, as said below
- fetch_counts: int32 [32, 16, 16], P('dp', 'shard'), may hold values from 0 to 16, as said below
- evict_rows: int32 [32, 16, 16, 16], P('dp', 'shard'), may hold values from 0 to 8191, as said below
- evict_from: int32 [32, 16, 16, 16], P('dp', 'shard'), may hold values from 0 to 255, as said below
- evict_counts: int32 [32, 16, 16], P('dp', 'shard'), may hold values from 0 to 16, as said below
Outputs:
- grad_first: bfloat16 [1024, 1024], P('shard')
- table_after: float32 [32, 16, 512, 384], P('dp', 'shard')
- fetched: float32 [32, 16, 16, 16, 384], P('dp', 'shard')
The draws below stay inside these ranges and needn't reach their ends.
Inputs may be any that keep to these rules, and one draw needn't show every extreme that they name: In each group home is a permutation; row r belongs to owner home[r] // 512. `fetch_rows`: every entry, live or not, names a row of the owner whose list it is in; no row is live both in a fetch list and in a write-back list of the same group. `fetch_counts`: in every group some owner gets 16 from every device. `evict_rows`: every entry names a row of the owner whose list it is in; live entries of a group are all different rows. `evict_from`: the entries of one device are all different. `evict_counts`: in every group some owner gets 16 from every device. `cache_state`: the last 128 entries of a row are positive. `table_state`: the last 128 entries of a row are positive.
All inputs are finite; a program needn't handle non-finite values.
Results may differ from the reference program's by a relative error of at most 0.0061.
Values sent between devices are 32-bit elements; how exact they have to be, the bound alone decides.
No kernel may reach another device: no remote copies, remote signals or barrier semaphores. Data moves between devices by JAX's collectives and lax.ppermute only.
A program may use at most 64 MiB of HBM per device.

```python
import math
import jax
import jax.numpy as jnp
import numpy as np
from jax import lax

EMBED_DIM = 128
MLP_WIDTH = 1024
FEATURES = 8
TOK_DEV = 1024
CAPACITY = 16
CACHE_ROWS = 256
TABLE_ROWS = 512
GROUP_ROWS = 8192
N_SHARD = 16
N_DP = 32


def state_block(key, rows):
    key_value, key_first, key_second = jax.random.split(key, 3)
    shape = (N_DP, N_SHARD, rows, EMBED_DIM)
    value = jax.random.normal(key_value, shape, jnp.float32)
    first = 0.1 * jax.random.normal(key_first, shape, jnp.float32)
    second = jnp.exp(jax.random.uniform(key_second, shape, jnp.float32, math.log(0.001), math.log(0.1)))
    return jnp.concatenate([value, first, second], axis=3)


def draw_cache_state(key, part):
    return state_block(jax.random.fold_in(key, 3), CACHE_ROWS)


def draw_table_state(key, part):
    return state_block(jax.random.fold_in(key, 5), TABLE_ROWS)


def busy_counts(key):
    key_base, key_busy = jax.random.split(key)
    base = jax.random.randint(key_base, (N_SHARD, N_SHARD), 0, CAPACITY + 1)
    busy = jax.random.randint(key_busy, (), 0, N_SHARD)
    column = jnp.arange(N_SHARD, dtype=jnp.int32)[None, :]
    return jnp.where(column == busy, CAPACITY, base).astype(jnp.int32)


def group_plan(key):
    key_home, key_order, key_evict, key_fetch, key_from = jax.random.split(key, 5)
    home = jax.random.permutation(key_home, GROUP_ROWS).astype(jnp.int32)
    inverse = jnp.argsort(home).astype(jnp.int32)
    orders = jax.vmap(lambda k: jax.random.permutation(k, TABLE_ROWS))(jax.random.split(key_order, N_SHARD)).astype(jnp.int32)
    owner = jnp.arange(N_SHARD, dtype=jnp.int32)[None, :, None]
    asker = jnp.arange(N_SHARD, dtype=jnp.int32)[:, None, None]
    within = jnp.arange(CAPACITY, dtype=jnp.int32)[None, None, :]
    position = asker * CAPACITY + within
    evict_slot = orders[owner, position]
    fetch_slot = orders[owner, N_SHARD * CAPACITY + position]
    evict_rows = inverse[owner * TABLE_ROWS + evict_slot].astype(jnp.int32)
    fetch_rows = inverse[owner * TABLE_ROWS + fetch_slot].astype(jnp.int32)
    sources = jax.vmap(lambda k: jax.random.permutation(k, CACHE_ROWS))(jax.random.split(key_from, N_SHARD))
    evict_from = sources.reshape(N_SHARD, N_SHARD, CAPACITY).astype(jnp.int32)
    return (home, fetch_rows, busy_counts(key_fetch), evict_rows, evict_from, busy_counts(key_evict))


def index_plan(key):
    keys = jax.random.split(jax.random.fold_in(key, 11), N_DP)
    return jax.vmap(group_plan)(keys)


def draw_home(key, part):
    return index_plan(key)[0]


def draw_fetch_rows(key, part):
    return index_plan(key)[1]


def draw_fetch_counts(key, part):
    return index_plan(key)[2]


def draw_evict_rows(key, part):
    return index_plan(key)[3]


def draw_evict_from(key, part):
    return index_plan(key)[4]


def draw_evict_counts(key, part):
    return index_plan(key)[5]


def plant(drawn, own_key, least, largest):
    dims = drawn.shape
    index_at = [jax.random.randint(jax.random.fold_in(own_key, axis), (), 0, dims[axis]) for axis in range(len(dims))]
    drawn = drawn.at[tuple(index_at)].set(least)
    longest = dims.index(max(dims))
    index_at[longest] = (index_at[longest] + 1) % dims[longest]
    return drawn.at[tuple(index_at)].set(largest)


def levels(own_key, extent, cuts, least, largest):
    gain, own = 1.0, jax.random.fold_in(own_key, 6)
    for axis_at, parts in cuts:
        steps = jnp.exp(jax.random.uniform(jax.random.fold_in(own, axis_at), (parts,), jnp.float32, least / len(cuts), largest / len(cuts)))
        gain = gain * jnp.repeat(steps, extent[axis_at] // parts).reshape([-1 if axis == axis_at else 1 for axis in range(len(extent))])
    return gain


def rank_bounds(number_of, slope):
    loads = [(1 << 20) // math.isqrt(rank ** slope) + 1 for rank in range(1, number_of + 1)]
    spread = 1 + sum(loads) // (1 << 30)
    return np.cumsum(np.array([max(1, weight // spread) for weight in loads]))


def skewed_ids(key, shape, count, slope):
    listing = rank_bounds(count, slope)
    pick = jax.random.randint(jax.random.fold_in(key, 1), shape, 0, int(listing[count - 1]))
    standing = jnp.searchsorted(jnp.asarray(listing, jnp.int32), pick, side="right")
    return jax.random.permutation(jax.random.fold_in(key, 2), count)[standing].astype(jnp.int32)


def noise(key, shape, scale, limit, shards=(), kind=jnp.bfloat16):
    factor_of = levels(key, shape, shards, -0.22, 0.18) if shards else 1.0
    values = jax.random.normal(key, shape, jnp.float32) * scale * factor_of
    return jnp.minimum(jnp.maximum(values, -limit), limit).astype(kind)


def setup_inputs(seed: int = 0) -> dict:
    arg_keys = jax.random.split(jax.random.key(seed), 13)
    return {
        "cache_state": draw_cache_state(jax.random.fold_in(arg_keys[12], 71), 0),
        "table_state": draw_table_state(jax.random.fold_in(arg_keys[12], 71), 0),
        "batch_idx": plant(skewed_ids(arg_keys[2], (N_DP, N_SHARD, TOK_DEV, FEATURES), CACHE_ROWS, 2), jax.random.fold_in(arg_keys[2], 3), 0, CACHE_ROWS - 1).astype(jnp.int32),
        "loss_grad": noise(arg_keys[3], (N_DP, N_SHARD, TOK_DEV), 1.0, 6.0, ((0, 32), (1, 16)), jnp.float32),
        "w_first": noise(arg_keys[4], (MLP_WIDTH, MLP_WIDTH), MLP_WIDTH ** -0.5, 0.1875),
        "head": noise(arg_keys[5], (MLP_WIDTH,), 1.0, 6.0, (), jnp.float32),
        "home": draw_home(jax.random.fold_in(arg_keys[12], 71), 0),
        "fetch_rows": draw_fetch_rows(jax.random.fold_in(arg_keys[12], 71), 0),
        "fetch_counts": draw_fetch_counts(jax.random.fold_in(arg_keys[12], 71), 0),
        "evict_rows": draw_evict_rows(jax.random.fold_in(arg_keys[12], 71), 0),
        "evict_from": draw_evict_from(jax.random.fold_in(arg_keys[12], 71), 0),
        "evict_counts": draw_evict_counts(jax.random.fold_in(arg_keys[12], 71), 0),
    }


beta_one = 0.9
beta_two = 0.999
learn_rate = 0.05
epsilon = 1e-08
bias_one = 1.0 - 0.9 ** 10
bias_two = 1.0 - 0.999 ** 10

def adam_rows(state, grads):
    value = state[:, :EMBED_DIM]
    first = state[:, EMBED_DIM:2 * EMBED_DIM]
    second = state[:, 2 * EMBED_DIM:]
    first = beta_one * first + (1.0 - beta_one) * grads
    second = beta_two * second + (1.0 - beta_two) * grads * grads
    value = value - learn_rate * (first / bias_one) / (jnp.sqrt(second / bias_two) + epsilon)
    return jnp.concatenate([value, first, second], axis=1)

def local_pass(cache, batch, loss, w_first, head):
    looked = jnp.take(cache[:, :EMBED_DIM], batch.reshape(-1), axis=0)
    inputs = looked.reshape(batch.shape[0], MLP_WIDTH).astype(jnp.bfloat16)
    pre = jnp.dot(inputs, w_first, preferred_element_type=jnp.float32)
    sigma = jax.nn.sigmoid(pre)
    delta = (loss[:, None] * head[None, :] * sigma * (1.0 + pre * (1.0 - sigma))).astype(jnp.bfloat16)
    term = lax.dot_general(inputs, delta, (((0,), (0,)), ((), ())), preferred_element_type=jnp.float32)
    back = lax.dot_general(delta, w_first, (((1,), (1,)), ((), ())), preferred_element_type=jnp.float32)
    grads = jax.ops.segment_sum(back.reshape(-1, EMBED_DIM), batch.reshape(-1), num_segments=cache.shape[0])
    return (term, adam_rows(cache, grads))

def settle(table_g, updated_g, home_g, ev_rows, ev_from, ev_counts, fe_rows, fe_counts):
    width = 3 * EMBED_DIM
    flat_table = table_g.reshape(GROUP_ROWS, width)
    within = jnp.arange(CAPACITY, dtype=jnp.int32)
    ev_live = within[None, None, :] < ev_counts[:, :, None]
    dest = jnp.where(ev_live, jnp.take(home_g, ev_rows, axis=0), GROUP_ROWS).astype(jnp.int32)
    source = jax.vmap(lambda rows, place: jnp.take(rows, place.reshape(-1), axis=0))(updated_g, ev_from)
    new_table = flat_table.at[dest.reshape(-1)].set(source.reshape(-1, width), mode='drop')
    fe_live = within[None, None, :] < fe_counts[:, :, None]
    place = jnp.take(home_g, fe_rows, axis=0).reshape(-1)
    got = jnp.take(flat_table, place, axis=0).reshape(N_SHARD, N_SHARD, CAPACITY, width)
    got = jnp.where(fe_live[..., None], got, jnp.zeros_like(got))
    return (new_table.reshape(N_SHARD, TABLE_ROWS, width), got)

def reference(cache_state, table_state, batch_idx, loss_grad, w_first, head, home, fetch_rows, fetch_counts, evict_rows, evict_from, evict_counts):
    count_all = N_DP * N_SHARD
    flat_cache = cache_state.reshape(count_all, CACHE_ROWS, 3 * EMBED_DIM)
    flat_batch = batch_idx.reshape(count_all, TOK_DEV, FEATURES)
    flat_loss = loss_grad.reshape(count_all, TOK_DEV)

    def step(total, item):
        term, updated = local_pass(item[0], item[1], item[2], w_first, head)
        return (total + term, updated)
    total, updated = lax.scan(step, jnp.zeros((MLP_WIDTH, MLP_WIDTH), jnp.float32), (flat_cache, flat_batch, flat_loss))
    grad_first = (total / math.sqrt(TOK_DEV * count_all)).astype(jnp.bfloat16)
    updated = updated.reshape(N_DP, N_SHARD, CACHE_ROWS, 3 * EMBED_DIM)
    table_after, fetched = jax.vmap(settle)(table_state, updated, home, evict_rows, evict_from, evict_counts, fetch_rows, fetch_counts)
    return (grad_first, table_after, fetched)
```

```python
import math

import jax
import jax.numpy as jnp
from jax import lax
from jax.experimental import pallas as pl
from jax.experimental.pallas import tpu as pltpu
from jax.sharding import PartitionSpec as P

beta_one = 0.9
beta_two = 0.999
learn_rate = 0.05
epsilon = 1e-08
bias_one = 1.0 - 0.9**10
bias_two = 1.0 - 0.999**10
NN = (((1,), (0,)), ((), ()))
NT = (((1,), (1,)), ((), ()))
TN = (((0,), (0,)), ((), ()))
side = 4


def full(shape):
    return pl.BlockSpec(shape, lambda j, o: tuple(0 for _ in shape))


def column(row):
    return jnp.transpose(jnp.broadcast_to(row, (8, row.shape[1])))[:, :1]


def onehot(batch_row, rows):
    shape = (rows, batch_row.shape[1])
    hit = lax.broadcasted_iota(jnp.int32, shape, 0) == batch_row
    return hit.astype(jnp.float32).astype(jnp.bfloat16)


def hidden(inputs, loss, head, w, delta_ref, grad_ref):
    pre = lax.dot_general(w, inputs, TN, preferred_element_type=jnp.float32)
    sigma = jax.nn.sigmoid(pre)
    delta = (loss * column(head) * sigma * (1.0 + pre * (1.0 - sigma))).astype(jnp.bfloat16)
    delta_ref[...] = delta
    grad_ref[...] = lax.dot_general(inputs, delta, NT, preferred_element_type=jnp.float32)


def first_kernel(order, cache_ref, batch_ref, loss_ref, head_ref, w_ref, grad_ref, delta_ref, inputs_ref):
    rows = cache_ref.shape[0]
    features = batch_ref.shape[0]
    embed = inputs_ref.shape[0] // features

    @pl.when(pl.program_id(0) == 0)
    def _():
        looked = jnp.transpose(cache_ref[...]).astype(jnp.bfloat16)
        for f in range(features):
            pick = onehot(batch_ref[f : f + 1, :], rows)
            inputs_ref[f * embed : (f + 1) * embed, :] = lax.dot_general(
                looked, pick, NN, preferred_element_type=jnp.float32
            ).astype(jnp.bfloat16)

    hidden(inputs_ref[...], loss_ref[...], head_ref[...], w_ref[...], delta_ref, grad_ref)


def second_kernel(order, inputs_ref, loss_ref, head_ref, w_ref, grad_ref, delta_ref):
    hidden(inputs_ref[...], loss_ref[...], head_ref[...], w_ref[...], delta_ref, grad_ref)


def forward_half(order, cache, batch_t, inputs, loss, head, w):
    samples = loss.shape[1]
    width = w.shape[0]
    half = width // 2
    block = half // 2
    steps = half // block
    tail_specs = [
        full((1, samples)),
        pl.BlockSpec((1, block), lambda j, o: (0, o[j])),
        pl.BlockSpec((width, block), lambda j, o: (0, o[j])),
    ]
    grad = jax.ShapeDtypeStruct((width, half), jnp.float32)
    delta = jax.ShapeDtypeStruct((half, samples), jnp.bfloat16)
    grad_spec = pl.BlockSpec((width, block), lambda j, o: (0, j))
    delta_spec = pl.BlockSpec((block, samples), lambda j, o: (j, 0))
    if inputs is None:
        rows = cache.shape[0]
        embed = cache.shape[1] // 3
        return pl.pallas_call(
            first_kernel,
            out_shape=(grad, delta, jax.ShapeDtypeStruct((width, samples), jnp.bfloat16)),
            grid_spec=pltpu.PrefetchScalarGridSpec(
                num_scalar_prefetch=1,
                grid=(steps,),
                in_specs=[pl.BlockSpec((rows, embed), lambda j, o: (0, 0)), full(batch_t.shape)] + tail_specs,
                out_specs=(grad_spec, delta_spec, full((width, samples))),
            ),
            name="forward_first",
        )(order, cache, batch_t, loss, head, w)
    return pl.pallas_call(
        second_kernel,
        out_shape=(grad, delta),
        grid_spec=pltpu.PrefetchScalarGridSpec(
            num_scalar_prefetch=1,
            grid=(steps,),
            in_specs=[full((width, samples))] + tail_specs,
            out_specs=(grad_spec, delta_spec),
        ),
        name="forward_second",
    )(order, inputs, loss, head, w)


def backward_kernel(where, cache_ref, batch_ref, delta_a, delta_b, w_a, w_b, sent_ref, acc_ref, upd_ref):
    rows, width = cache_ref.shape
    embed = width // 3
    step = pl.program_id(0)
    back = lax.dot_general(w_a[...], delta_a[...], NN, preferred_element_type=jnp.float32)
    back += lax.dot_general(w_b[...], delta_b[...], NN, preferred_element_type=jnp.float32)
    total = None
    for k in range(w_a.shape[0] // embed):
        part = back[k * embed : (k + 1) * embed]
        high = part.astype(jnp.bfloat16)
        low = (part - high.astype(jnp.float32)).astype(jnp.bfloat16)
        pick = onehot(batch_ref[0, k : k + 1, :], rows)
        add = lax.dot_general(jnp.concatenate([high, low], 0), pick, NT, preferred_element_type=jnp.float32)
        total = add if total is None else total + add

    @pl.when(step == 0)
    def _():
        acc_ref[...] = total

    @pl.when(step > 0)
    def _():
        acc_ref[...] += total

    @pl.when(step == pl.num_programs(0) - 1)
    def _():
        grads = jnp.transpose(acc_ref[:embed, :] + acc_ref[embed:, :])
        value = cache_ref[:, :embed]
        first = cache_ref[:, embed : 2 * embed]
        second = cache_ref[:, 2 * embed :]
        first = beta_one * first + (1.0 - beta_one) * grads
        second = beta_two * second + (1.0 - beta_two) * grads * grads
        upd_ref[:, :embed] = value - learn_rate * (first / bias_one) / (jnp.sqrt(second / bias_two) + epsilon)
        upd_ref[:, embed : 2 * embed] = first
        upd_ref[:, 2 * embed :] = second

        def move(i, carry):
            for u in range(8):
                r = i * 8 + u
                sent_ref[pl.ds(r, 1), :] = upd_ref[pl.ds(where[r], 1), :]
            return carry

        lax.fori_loop(0, sent_ref.shape[0] // 8, move, 0)


def backward(where, cache, batch_t, delta_a, delta_b, w):
    rows, width3 = cache.shape
    embed = width3 // 3
    features, samples = batch_t.shape
    width = w.shape[0]
    half = width // 2
    steps = features // 2
    count = where.shape[0] - 2
    return pl.pallas_call(
        backward_kernel,
        out_shape=jax.ShapeDtypeStruct((count, width3), jnp.float32),
        grid_spec=pltpu.PrefetchScalarGridSpec(
            num_scalar_prefetch=1,
            grid=(steps,),
            in_specs=[
                full((rows, width3)),
                pl.BlockSpec((1, 2, samples), lambda j, o: (j, 0, 0)),
                full((half, samples)),
                full((half, samples)),
                pl.BlockSpec((2 * embed, half), lambda j, o: (j, o[count])),
                pl.BlockSpec((2 * embed, half), lambda j, o: (j, o[count + 1])),
            ],
            out_specs=full((count, width3)),
            scratch_shapes=[pltpu.VMEM((2 * embed, rows), jnp.float32), pltpu.VMEM((rows, width3), jnp.float32)],
        ),
        name="backward",
    )(where, cache, batch_t.reshape(steps, 2, samples), delta_a, delta_b, w, w)


def swap_pairs():
    return [(d, d ^ 1) for d in range(2 * side * side)]


def ring_pairs(step_x, step_y):
    return [
        ((x * side + y) * 2 + c, (((x + step_x) % side) * side + (y + step_y) % side) * 2 + c)
        for x in range(side)
        for y in range(side)
        for c in range(2)
    ]


def pick_block(a, i, axis):
    return lax.dynamic_index_in_dim(a, i & (side - 1), axis, keepdims=False)


def spread(a, i, axis, along_x):
    total = pick_block(a, i, axis)
    parts = [
        lax.ppermute(pick_block(a, i + s, axis), "dp", ring_pairs(s, 0) if along_x else ring_pairs(0, s))
        for s in range(1, side)
    ]
    return total + parts[0] + parts[1] + parts[2]


def reduce_gradient(send, keep, place):
    x, y = place >> 3, (place >> 1) & (side - 1)
    group = lax.axis_size("shard")
    mine = keep + lax.ppermute(send, "dp", swap_pairs())
    width, half = mine.shape
    mine = mine.reshape(group, 2, side, width // (group * 2 * side), side, half // side)
    even, odd = mine[:, 0], mine[:, 1]
    even = spread(even, x, 3, True)
    odd = spread(odd, y, 1, False)
    even = spread(even, y, 1, False)
    odd = spread(odd, x, 2, True)
    both = jnp.stack([even, odd], 1)
    both = lax.all_to_all(both, "shard", split_axis=0, concat_axis=0, tiled=True)
    return jnp.sum(both, 0)


def local(
    cache_state,
    table_state,
    batch_idx,
    loss_grad,
    w_first,
    head,
    home,
    fetch_rows,
    fetch_counts,
    evict_rows,
    evict_from,
    evict_counts,
):
    group = lax.axis_size("shard")
    devices = lax.axis_size("dp")
    place = lax.axis_index("dp").astype(jnp.uint32)
    core = (place & 1).astype(jnp.int32)
    cache = cache_state[0, 0]
    table = table_state[0, 0]
    batch_t = batch_idx[0, 0].T
    loss = loss_grad[0]
    home_map = home[0]
    wanted = fetch_rows[0, 0]
    gone = evict_rows[0, 0]
    width = cache.shape[1]
    table_rows = table.shape[0]
    capacity = wanted.shape[1]
    samples = loss.shape[1]
    mlp_width = w_first.shape[0]
    within = jnp.arange(capacity, dtype=jnp.int32)[None, :]
    wanted_live = within < fetch_counts[0, 0][:, None]
    gone_live = within < evict_counts[0, 0][:, None]

    slots = jnp.take(home_map, jnp.concatenate([wanted, gone], 1), axis=0) % table_rows
    live = jnp.concatenate([jnp.ones_like(wanted_live), gone_live], 1)
    asked = lax.all_to_all(
        jnp.where(live, slots, table_rows), "shard", split_axis=0, concat_axis=0, tiled=True
    )
    got_slots = asked[:, capacity:]
    arrived = lax.all_to_all(
        jnp.take(table, asked[:, :capacity], axis=0), "shard", split_axis=0, concat_axis=0, tiled=True
    )

    far = 1 - core
    order = jnp.arange(2, dtype=jnp.int32)
    send, delta_a, inputs = forward_half(order + 2 * far, cache, batch_t, None, loss, head[None], w_first)
    keep, delta_b = forward_half(order + 2 * core, cache, batch_t, inputs, loss, head[None], w_first)
    where = jnp.concatenate([evict_from[0, 0].reshape(-1), jnp.stack([far, core]).astype(jnp.int32)])
    sent_rows = backward(where, cache, batch_t, delta_a, delta_b, w_first).reshape(group, capacity, width)
    got_rows = lax.all_to_all(sent_rows, "shard", split_axis=0, concat_axis=0, tiled=True)
    new_table = table.at[got_slots.reshape(-1)].set(got_rows.reshape(-1, width), mode="drop")
    fetched = jnp.where(wanted_live[:, :, None], arrived, jnp.zeros_like(arrived))

    mine = reduce_gradient(send, keep, place)
    scale = 1.0 / math.sqrt(samples * group * devices)
    every = lax.all_to_all(
        jnp.broadcast_to(mine[None], (devices,) + mine.shape), "dp", split_axis=0, concat_axis=0, tiled=True
    )
    rows, columns = mine.shape[1:]
    every = every.reshape(side, side, 2, 2, rows, columns).transpose(3, 1, 4, 2, 0, 5)
    grad_first = (every.reshape(mlp_width // group, mlp_width) * scale).astype(jnp.bfloat16)
    return (grad_first, new_table[None, None], fetched[None, None])


def solution(mesh):
    placed = (
        P("dp", "shard", None, None),
        P("dp", "shard", None, None),
        P("dp", "shard", None, None),
        P("dp", "shard", None),
        P(),
        P(),
        P("dp", None),
        P("dp", "shard", None, None),
        P("dp", "shard", None),
        P("dp", "shard", None, None),
        P("dp", "shard", None, None),
        P("dp", "shard", None),
    )
    return jax.shard_map(
        local,
        mesh=mesh,
        in_specs=placed,
        out_specs=(
            P("shard", None),
            P("dp", "shard", None, None),
            P("dp", "shard", None, None, None),
        ),
        check_vma=False,
    )
```

```python
import math

import jax
import jax.numpy as jnp
from jax import lax
from jax.experimental import pallas as pl
from jax.experimental.pallas import tpu as pltpu
from jax.sharding import PartitionSpec as P


beta_one = 0.9
beta_two = 0.999
learn_rate = 0.05
epsilon = 1e-08
bias_one = 1.0 - 0.9**10
bias_two = 1.0 - 0.999**10
NN = (((1,), (0,)), ((), ()))
NT = (((1,), (1,)), ((), ()))
TN = (((0,), (0,)), ((), ()))
side = 4


def full(shape):
    return pl.BlockSpec(shape, lambda j, o: tuple(0 for _ in shape))


def column(row):
    return jnp.transpose(jnp.broadcast_to(row, (8, row.shape[1])))[:, :1]


def onehot(batch_row, rows):
    shape = (rows, batch_row.shape[1])
    hit = lax.broadcasted_iota(jnp.int32, shape, 0) == batch_row
    return hit.astype(jnp.float32).astype(jnp.bfloat16)


def hidden(inputs, loss, head, w, delta_ref):
    pre = lax.dot_general(w, inputs, TN, preferred_element_type=jnp.float32)
    sigma = jax.nn.sigmoid(pre)
    delta = (loss * column(head) * sigma * (1.0 + pre * (1.0 - sigma))).astype(jnp.bfloat16)
    delta_ref[...] = delta
    return lax.dot_general(inputs, delta, NT, preferred_element_type=jnp.float32)


def store_pieces(grad, grad_ref, plus_ref):
    across, down, owners, rows, columns = grad_ref.shape
    for x in range(across):
        for y in range(down):
            for z in range(owners):
                top = (z * down + y) * rows
                piece = grad[top : top + rows, x * columns : (x + 1) * columns]
                grad_ref[x, y, z] = piece if plus_ref is None else piece + plus_ref[x, y, z]


def first_kernel(cores, cache_ref, batch_ref, loss_ref, head_ref, w_ref, grad_ref, delta_ref, inputs_ref):
    rows = cache_ref.shape[0]
    features = batch_ref.shape[0]
    embed = inputs_ref.shape[0] // features

    @pl.when(pl.program_id(0) == 0)
    def _():
        looked = jnp.transpose(cache_ref[...]).astype(jnp.bfloat16)
        for f in range(features):
            pick = onehot(batch_ref[f : f + 1, :], rows)
            inputs_ref[f * embed : (f + 1) * embed, :] = lax.dot_general(
                looked, pick, NN, preferred_element_type=jnp.float32
            ).astype(jnp.bfloat16)

    grad = hidden(inputs_ref[...], loss_ref[...], head_ref[...], w_ref[...], delta_ref)
    store_pieces(grad, grad_ref, None)


def second_kernel(cores, plus_ref, inputs_ref, loss_ref, head_ref, w_ref, grad_ref, delta_ref):
    grad = hidden(inputs_ref[...], loss_ref[...], head_ref[...], w_ref[...], delta_ref)
    store_pieces(grad, grad_ref, plus_ref)


def forward_half(cores, owners, cache, batch_t, partner, inputs, loss, head, w):
    samples = loss.shape[1]
    width = w.shape[0]
    half = width // 2
    steps = 2
    block = half // steps
    here = 0 if inputs is None else 1
    tail_specs = [
        full((1, samples)),
        pl.BlockSpec((1, block), lambda j, c: (0, steps * c[here] + j)),
        pl.BlockSpec((width, block), lambda j, c: (0, steps * c[here] + j)),
    ]
    pieces = (side, side, owners, width // (owners * side), half // side)
    grad = jax.ShapeDtypeStruct(pieces, jnp.float32)
    delta = jax.ShapeDtypeStruct((half, samples), jnp.bfloat16)
    grad_spec = pl.BlockSpec((side // steps,) + pieces[1:], lambda j, c: (j, 0, 0, 0, 0))
    delta_spec = pl.BlockSpec((block, samples), lambda j, c: (j, 0))
    if inputs is None:
        rows = cache.shape[0]
        embed = cache.shape[1] // 3
        return pl.pallas_call(
            first_kernel,
            out_shape=(grad, delta, jax.ShapeDtypeStruct((width, samples), jnp.bfloat16)),
            grid_spec=pltpu.PrefetchScalarGridSpec(
                num_scalar_prefetch=1,
                grid=(steps,),
                in_specs=[pl.BlockSpec((rows, embed), lambda j, c: (0, 0)), full(batch_t.shape)] + tail_specs,
                out_specs=(grad_spec, delta_spec, full((width, samples))),
            ),
            name="forward_first",
        )(cores, cache, batch_t, loss, head, w)
    return pl.pallas_call(
        second_kernel,
        out_shape=(grad, delta),
        grid_spec=pltpu.PrefetchScalarGridSpec(
            num_scalar_prefetch=1,
            grid=(steps,),
            in_specs=[grad_spec, full((width, samples))] + tail_specs,
            out_specs=(grad_spec, delta_spec),
        ),
        name="forward_second",
    )(cores, partner, inputs, loss, head, w)


def backward_kernel(
    cores, asked, leaving, cache_ref, table_ref, batch_ref, delta_a, delta_b, w_a, w_b, sent_ref, acc_ref, upd_ref
):
    rows, width = cache_ref.shape
    embed = width // 3
    owners, capacity = leaving.shape
    step = pl.program_id(0)
    back = lax.dot_general(w_a[...], delta_a[...], NN, preferred_element_type=jnp.float32)
    back += lax.dot_general(w_b[...], delta_b[...], NN, preferred_element_type=jnp.float32)
    total = None
    for k in range(w_a.shape[0] // embed):
        part = back[k * embed : (k + 1) * embed]
        high = part.astype(jnp.bfloat16)
        low = (part - high.astype(jnp.float32)).astype(jnp.bfloat16)
        pick = onehot(batch_ref[pl.ds(step * (w_a.shape[0] // embed) + k, 1), :], rows)
        add = lax.dot_general(jnp.concatenate([high, low], 0), pick, NT, preferred_element_type=jnp.float32)
        total = add if total is None else total + add

    @pl.when(step == 0)
    def _():
        acc_ref[...] = total

        def fetch(i, carry):
            for k in range(capacity):
                row = table_ref[pl.ds(asked[i, k], 1), :]
                for p in range(3):
                    at = p * capacity + k
                    sent_ref[i, at : at + 1, :] = row[:, p * embed : (p + 1) * embed]
            return carry

        lax.fori_loop(0, owners, fetch, 0)

    @pl.when(step > 0)
    def _():
        acc_ref[...] += total

    @pl.when(step == pl.num_programs(0) - 1)
    def _():
        grads = jnp.transpose(acc_ref[:embed, :] + acc_ref[embed:, :])
        value = cache_ref[:, :embed]
        first = cache_ref[:, embed : 2 * embed]
        second = cache_ref[:, 2 * embed :]
        first = beta_one * first + (1.0 - beta_one) * grads
        second = beta_two * second + (1.0 - beta_two) * grads * grads
        upd_ref[:, :embed] = value - learn_rate * (first / bias_one) / (jnp.sqrt(second / bias_two) + epsilon)
        upd_ref[:, embed : 2 * embed] = first
        upd_ref[:, 2 * embed :] = second

        def evict(i, carry):
            for k in range(capacity):
                row = upd_ref[pl.ds(leaving[i, k], 1), :]
                for p in range(3):
                    at = (3 + p) * capacity + k
                    sent_ref[i, at : at + 1, :] = row[:, p * embed : (p + 1) * embed]
            return carry

        lax.fori_loop(0, owners, evict, 0)


def backward(cores, asked, leaving, cache, table, batch_t, delta_a, delta_b, w):
    rows, width3 = cache.shape
    embed = width3 // 3
    features, samples = batch_t.shape
    width = w.shape[0]
    half = width // 2
    steps = features // 2
    owners, capacity = leaving.shape
    fixed = lambda shape: pl.BlockSpec(shape, lambda j, c, a, e: tuple(0 for _ in shape))
    return pl.pallas_call(
        backward_kernel,
        out_shape=jax.ShapeDtypeStruct((owners, 7 * capacity, embed), jnp.float32),
        grid_spec=pltpu.PrefetchScalarGridSpec(
            num_scalar_prefetch=3,
            grid=(steps,),
            in_specs=[
                fixed(cache.shape),
                fixed(table.shape),
                fixed(batch_t.shape),
                fixed((half, samples)),
                fixed((half, samples)),
                pl.BlockSpec((2 * embed, half), lambda j, c, a, e: (j, c[0])),
                pl.BlockSpec((2 * embed, half), lambda j, c, a, e: (j, c[1])),
            ],
            out_specs=fixed((owners, 6 * capacity, embed)),
            scratch_shapes=[pltpu.VMEM((2 * embed, rows), jnp.float32), pltpu.VMEM((rows, width3), jnp.float32)],
        ),
        name="backward",
    )(cores, asked, leaving, cache, table, batch_t, delta_a, delta_b, w, w)


def total_kernel(pieces_ref, sent_ref, out_ref):
    total = pieces_ref[0]
    for i in range(1, pieces_ref.shape[0]):
        total += pieces_ref[i]
    out_ref[...] = total


def add_total(pieces, sent):
    count, owners, rows, columns = pieces.shape
    step = owners // 4
    return pl.pallas_call(
        total_kernel,
        out_shape=jax.ShapeDtypeStruct(sent.shape, sent.dtype),
        grid=(owners // step,),
        in_specs=[
            pl.BlockSpec((count, step, rows, columns), lambda j: (0, j, 0, 0)),
            pl.BlockSpec(memory_space=pl.ANY),
        ],
        out_specs=pl.BlockSpec((step, rows, columns), lambda j: (j, sent.shape[1] // rows - 1, 0)),
        input_output_aliases={1: 0},
        name="total",
    )(pieces, sent)


def swap_pairs():
    return [(d, d ^ 1) for d in range(2 * side * side)]


def planes():
    return [[2 * chip + c for chip in range(side * side)] for c in range(2)]


def local(
    cache_state,
    table_state,
    batch_idx,
    loss_grad,
    w_first,
    head,
    home,
    fetch_rows,
    fetch_counts,
    evict_rows,
    evict_from,
    evict_counts,
):
    group = lax.axis_size("shard")
    devices = lax.axis_size("dp")
    place = lax.axis_index("dp").astype(jnp.uint32)
    core = (place & 1).astype(jnp.int32)
    cache = cache_state[0, 0]
    table = table_state[0, 0]
    batch_t = batch_idx[0, 0].T
    loss = loss_grad[0]
    home_map = home[0]
    wanted = fetch_rows[0, 0]
    gone = evict_rows[0, 0]
    width = cache.shape[1]
    table_rows = table.shape[0]
    capacity = wanted.shape[1]
    samples = loss.shape[1]
    mlp_width = w_first.shape[0]
    within = jnp.arange(capacity, dtype=jnp.int32)[None, :]
    wanted_live = within < fetch_counts[0, 0][:, None]
    gone_live = within < evict_counts[0, 0][:, None]

    slots = jnp.take(home_map, jnp.concatenate([wanted, gone], 1), axis=0) % table_rows
    live = jnp.concatenate([jnp.ones_like(wanted_live), gone_live], 1)
    asked = lax.all_to_all(
        jnp.where(live, slots, table_rows), "shard", split_axis=0, concat_axis=0, tiled=True
    )
    got_slots = asked[:, capacity:]

    cores = jnp.stack([1 - core, core])
    head_row = head[None]
    send, delta_a, inputs = forward_half(cores, group, cache, batch_t, None, None, loss, head_row, w_first)
    partner = lax.ppermute(send, "dp", swap_pairs())
    partner = pltpu.with_memory_space_constraint(partner, pltpu.HBM)
    chip, delta_b = forward_half(cores, group, None, None, partner, inputs, loss, head_row, w_first)
    plane = side * side
    pieces = chip.reshape((plane,) + chip.shape[2:])
    pieces = lax.all_to_all(
        pieces, "dp", split_axis=0, concat_axis=0, axis_index_groups=planes(), tiled=True
    )
    sent = backward(cores, asked, evict_from[0, 0], cache, table, batch_t, delta_a, delta_b, w_first)
    sent = add_total(pltpu.with_memory_space_constraint(pieces, pltpu.HBM), sent)
    got = lax.all_to_all(sent, "shard", split_axis=0, concat_axis=0, tiled=True)
    embed = width // 3
    got = got.reshape(group, 7, capacity, embed)
    mine = jnp.sum(got[:, 6], 0)
    came = got[:, 3:6].transpose(0, 2, 1, 3).reshape(-1, width)
    new_table = table.at[got_slots.reshape(-1)].set(came, mode="drop")
    arrived = got[:, :3].transpose(0, 2, 1, 3).reshape(group, capacity, width)
    fetched = jnp.where(wanted_live[:, :, None], arrived, 0.0)
    scale = 1.0 / math.sqrt(samples * group * devices)
    every = lax.all_to_all(
        jnp.broadcast_to(mine[None], (devices,) + mine.shape), "dp", split_axis=0, concat_axis=0, tiled=True
    )
    every = every.reshape((side, side, 2) + mine.shape).transpose(1, 3, 2, 0, 4)
    grad_first = (every.reshape(mlp_width // group, mlp_width) * scale).astype(jnp.bfloat16)
    return (grad_first, new_table[None, None], fetched[None, None])


def solution(mesh):
    placed = (
        P("dp", "shard", None, None),
        P("dp", "shard", None, None),
        P("dp", "shard", None, None),
        P("dp", "shard", None),
        P(),
        P(),
        P("dp", None),
        P("dp", "shard", None, None),
        P("dp", "shard", None),
        P("dp", "shard", None, None),
        P("dp", "shard", None, None),
        P("dp", "shard", None),
    )

    return jax.shard_map(
        local,
        mesh=mesh,
        in_specs=placed,
        out_specs=(
            P("shard", None),
            P("dp", "shard", None, None),
            P("dp", "shard", None, None, None),
        ),
        check_vma=False,
    )
```

```python
import functools
import math

import jax
import jax.numpy as jnp
from jax import lax
from jax.experimental import pallas as pl
from jax.experimental.pallas import tpu as pltpu
from jax.sharding import PartitionSpec as P


beta_one = 0.9
beta_two = 0.999
learn_rate = 0.05
epsilon = 1e-08
bias_one = 1.0 - 0.9**10
bias_two = 1.0 - 0.999**10
NN = (((1,), (0,)), ((), ()))
NT = (((1,), (1,)), ((), ()))
TN = (((0,), (0,)), ((), ()))
side = 4


def full(shape):
    return pl.BlockSpec(shape, lambda j, o: tuple(0 for _ in shape))


def column(row):
    return jnp.transpose(jnp.broadcast_to(row, (8, row.shape[1])))[:, :1]


def onehot(batch_row, rows):
    shape = (rows, batch_row.shape[1])
    hit = lax.broadcasted_iota(jnp.int32, shape, 0) == batch_row
    return hit.astype(jnp.float32).astype(jnp.bfloat16)


def hidden(inputs, loss, head, w, delta_ref):
    pre = lax.dot_general(w, inputs, TN, preferred_element_type=jnp.float32)
    sigma = jax.nn.sigmoid(pre)
    delta = (loss * column(head) * sigma * (1.0 + pre * (1.0 - sigma))).astype(jnp.bfloat16)
    delta_ref[...] = delta
    return lax.dot_general(inputs, delta, NT, preferred_element_type=jnp.float32)


def store_pieces(grad, grad_ref, plus_ref):
    across, down, owners, rows, columns = grad_ref.shape
    for x in range(across):
        for y in range(down):
            for z in range(owners):
                top = (z * down + y) * rows
                piece = grad[top : top + rows, x * columns : (x + 1) * columns]
                grad_ref[x, y, z] = piece if plus_ref is None else piece + plus_ref[x, y, z]


def first_kernel(cores, cache_ref, batch_ref, loss_ref, head_ref, w_ref, grad_ref, delta_ref, inputs_ref):
    rows = cache_ref.shape[0]
    features = batch_ref.shape[0]
    embed = inputs_ref.shape[0] // features

    @pl.when(pl.program_id(0) == 0)
    def _():
        looked = jnp.transpose(cache_ref[...]).astype(jnp.bfloat16)
        for f in range(features):
            pick = onehot(batch_ref[f : f + 1, :], rows)
            inputs_ref[f * embed : (f + 1) * embed, :] = lax.dot_general(
                looked, pick, NN, preferred_element_type=jnp.float32
            ).astype(jnp.bfloat16)

    grad = hidden(inputs_ref[...], loss_ref[...], head_ref[...], w_ref[...], delta_ref)
    store_pieces(grad, grad_ref, None)


def second_kernel(cores, plus_all, inputs_ref, loss_ref, head_ref, w_ref, grad_ref, delta_ref):
    grad = hidden(inputs_ref[...], loss_ref[...], head_ref[...], w_ref[...], delta_ref)
    across = grad_ref.shape[0]
    store_pieces(grad, grad_ref, plus_all.at[pl.ds(pl.program_id(0) * across, across)])


def forward_half(cores, owners, cache, batch_t, partner, inputs, loss, head, w):
    samples = loss.shape[1]
    width = w.shape[0]
    half = width // 2
    steps = 2
    block = half // steps
    here = 0 if inputs is None else 1
    tail_specs = [
        full((1, samples)),
        pl.BlockSpec((1, block), lambda j, c: (0, steps * c[here] + j)),
        pl.BlockSpec((width, block), lambda j, c: (0, steps * c[here] + j)),
    ]
    pieces = (side, side, owners, width // (owners * side), half // side)
    grad = jax.ShapeDtypeStruct(pieces, jnp.float32)
    delta = jax.ShapeDtypeStruct((half, samples), jnp.bfloat16)
    grad_spec = pl.BlockSpec((side // steps,) + pieces[1:], lambda j, c: (j, 0, 0, 0, 0))
    delta_spec = pl.BlockSpec((block, samples), lambda j, c: (j, 0))
    if inputs is None:
        rows = cache.shape[0]
        embed = cache.shape[1] // 3
        return pl.pallas_call(
            first_kernel,
            out_shape=(grad, delta, jax.ShapeDtypeStruct((width, samples), jnp.bfloat16)),
            grid_spec=pltpu.PrefetchScalarGridSpec(
                num_scalar_prefetch=1,
                grid=(steps,),
                in_specs=[pl.BlockSpec((rows, embed), lambda j, c: (0, 0)), full(batch_t.shape)] + tail_specs,
                out_specs=(grad_spec, delta_spec, full((width, samples))),
            ),
            name="forward_first",
        )(cores, cache, batch_t, loss, head, w)
    return pl.pallas_call(
        second_kernel,
        out_shape=(grad, delta),
        grid_spec=pltpu.PrefetchScalarGridSpec(
            num_scalar_prefetch=1,
            grid=(steps,),
            in_specs=[pl.BlockSpec(memory_space=pltpu.VMEM), full((width, samples))] + tail_specs,
            out_specs=(grad_spec, delta_spec),
        ),
        name="forward_second",
    )(cores, partner, inputs, loss, head, w)


def backward_kernel(
    cores, asked, leaving, cache_ref, table_ref, batch_ref, delta_a, delta_b, w_a, w_b, sent_ref, acc_ref, upd_ref
):
    rows, width = cache_ref.shape
    embed = width // 3
    owners, capacity = leaving.shape
    step = pl.program_id(0)
    back = lax.dot_general(w_a[...], delta_a[...], NN, preferred_element_type=jnp.float32)
    back += lax.dot_general(w_b[...], delta_b[...], NN, preferred_element_type=jnp.float32)
    total = None
    for k in range(w_a.shape[0] // embed):
        part = back[k * embed : (k + 1) * embed]
        high = part.astype(jnp.bfloat16)
        low = (part - high.astype(jnp.float32)).astype(jnp.bfloat16)
        pick = onehot(batch_ref[pl.ds(step * (w_a.shape[0] // embed) + k, 1), :], rows)
        add = lax.dot_general(jnp.concatenate([high, low], 0), pick, NT, preferred_element_type=jnp.float32)
        total = add if total is None else total + add

    @pl.when(step == 0)
    def _():
        acc_ref[...] = total

        def fetch(i, carry):
            for k in range(capacity):
                row = table_ref[pl.ds(asked[i, k], 1), :]
                for p in range(3):
                    at = p * capacity + k
                    sent_ref[i, at : at + 1, :] = row[:, p * embed : (p + 1) * embed]
            return carry

        lax.fori_loop(0, owners, fetch, 0)

    @pl.when(step > 0)
    def _():
        acc_ref[...] += total

    @pl.when(step == pl.num_programs(0) - 1)
    def _():
        grads = jnp.transpose(acc_ref[:embed, :] + acc_ref[embed:, :])
        value = cache_ref[:, :embed]
        first = cache_ref[:, embed : 2 * embed]
        second = cache_ref[:, 2 * embed :]
        first = beta_one * first + (1.0 - beta_one) * grads
        second = beta_two * second + (1.0 - beta_two) * grads * grads
        upd_ref[:, :embed] = value - learn_rate * (first / bias_one) / (jnp.sqrt(second / bias_two) + epsilon)
        upd_ref[:, embed : 2 * embed] = first
        upd_ref[:, 2 * embed :] = second

        def evict(i, carry):
            for k in range(capacity):
                row = upd_ref[pl.ds(leaving[i, k], 1), :]
                for p in range(3):
                    at = (3 + p) * capacity + k
                    sent_ref[i, at : at + 1, :] = row[:, p * embed : (p + 1) * embed]
            return carry

        lax.fori_loop(0, owners, evict, 0)


def backward(cores, asked, leaving, cache, table, batch_t, delta_a, delta_b, w):
    rows, width3 = cache.shape
    embed = width3 // 3
    features, samples = batch_t.shape
    width = w.shape[0]
    half = width // 2
    steps = features // 2
    owners, capacity = leaving.shape
    fixed = lambda shape: pl.BlockSpec(shape, lambda j, c, a, e: tuple(0 for _ in shape))
    return pl.pallas_call(
        backward_kernel,
        out_shape=jax.ShapeDtypeStruct((owners, 7 * capacity, embed), jnp.float32),
        grid_spec=pltpu.PrefetchScalarGridSpec(
            num_scalar_prefetch=3,
            grid=(steps,),
            in_specs=[
                fixed(cache.shape),
                fixed(table.shape),
                fixed(batch_t.shape),
                fixed((half, samples)),
                fixed((half, samples)),
                pl.BlockSpec((2 * embed, half), lambda j, c, a, e: (j, c[0])),
                pl.BlockSpec((2 * embed, half), lambda j, c, a, e: (j, c[1])),
            ],
            out_specs=fixed((owners, 6 * capacity, embed)),
            scratch_shapes=[pltpu.VMEM((2 * embed, rows), jnp.float32), pltpu.VMEM((rows, width3), jnp.float32)],
        ),
        name="backward",
    )(cores, asked, leaving, cache, table, batch_t, delta_a, delta_b, w, w)


def total_kernel(pieces_ref, sent_ref, out_ref):
    owners = out_ref.shape[0]
    here = pl.ds(pl.program_id(0) * owners, owners)
    total = pieces_ref[0, here]
    for i in range(1, pieces_ref.shape[0]):
        total += pieces_ref[i, here]
    out_ref[...] = total


def add_total(pieces, sent):
    _, owners, rows, columns = pieces.shape
    step = owners // 4
    return pl.pallas_call(
        total_kernel,
        out_shape=jax.ShapeDtypeStruct(sent.shape, sent.dtype),
        grid=(owners // step,),
        in_specs=[
            pl.BlockSpec(memory_space=pltpu.VMEM),
            pl.BlockSpec(memory_space=pl.ANY),
        ],
        out_specs=pl.BlockSpec((step, rows, columns), lambda j: (j, sent.shape[1] // rows - 1, 0)),
        input_output_aliases={1: 0},
        name="total",
    )(pieces, sent)


def lookup_kernel(home_ref, wanted_ref, gone_ref, counts_ref, out_ref, *, table_rows):
    owners, capacity = wanted_ref.shape

    def look(i, carry):
        count = counts_ref[0, i]
        for k in range(capacity):
            out_ref[i, k] = home_ref[0, wanted_ref[i, k]] & (table_rows - 1)
            slot = home_ref[0, gone_ref[i, k]] & (table_rows - 1)
            out_ref[i, capacity + k] = jnp.where(k < count, slot, table_rows)
        return carry

    lax.fori_loop(0, owners, look, 0)


def lookup(home, wanted, gone, counts, table_rows):
    owners, capacity = wanted.shape
    scalar = pl.BlockSpec(memory_space=pltpu.SMEM)
    return pl.pallas_call(
        functools.partial(lookup_kernel, table_rows=table_rows),
        out_shape=jax.ShapeDtypeStruct((owners, 2 * capacity), jnp.int32),
        in_specs=[scalar] * 4,
        out_specs=scalar,
        name="lookup",
    )(home, wanted, gone, counts)


def share_kernel(got_ref, out_ref):
    rows = out_ref.shape[1]
    last = pl.ds(got_ref.shape[1] - rows, rows)
    total = got_ref[0, last]
    for i in range(1, got_ref.shape[0]):
        total += got_ref[i, last]
    for d in range(out_ref.shape[0]):
        out_ref[d] = total


def share_total(got, rows, devices):
    return pl.pallas_call(
        share_kernel,
        out_shape=jax.ShapeDtypeStruct((devices, rows, got.shape[2]), got.dtype),
        in_specs=[pl.BlockSpec(memory_space=pltpu.VMEM)],
        name="share_total",
    )(got)


def settle_kernel(asked_ref, counts_ref, got_ref, table_ref, new_ref, fetched_ref, rows_ref):
    owners, both = asked_ref.shape
    capacity = both // 2
    embed = got_ref.shape[2]
    table_rows = table_ref.shape[0]
    for p in range(3):
        rows_ref[p, :table_rows] = table_ref[:, p * embed : (p + 1) * embed]

    def place(i, carry):
        for k in range(capacity):
            slot = asked_ref[i, capacity + k]
            for p in range(3):
                at = (3 + p) * capacity + k
                rows_ref[p, pl.ds(slot, 1), :] = got_ref[i, at : at + 1, :]
        live = lax.broadcasted_iota(jnp.int32, (capacity, embed), 0) < counts_ref[0, i]
        for p in range(3):
            block = got_ref[i, p * capacity : (p + 1) * capacity, :]
            fetched_ref[i, :, p * embed : (p + 1) * embed] = jnp.where(live, block, 0.0)
        return carry

    lax.fori_loop(0, owners, place, 0)
    for p in range(3):
        new_ref[:, p * embed : (p + 1) * embed] = rows_ref[p, :table_rows]


def settle(asked, counts, got, table):
    owners, both = asked.shape
    table_rows, width = table.shape
    scalar = pl.BlockSpec(memory_space=pltpu.SMEM)
    whole = pl.BlockSpec(memory_space=pltpu.VMEM)
    return pl.pallas_call(
        settle_kernel,
        out_shape=(
            jax.ShapeDtypeStruct(table.shape, table.dtype),
            jax.ShapeDtypeStruct((owners, both // 2, width), table.dtype),
        ),
        in_specs=[scalar, scalar, whole, pl.BlockSpec(table.shape)],
        out_specs=(pl.BlockSpec(table.shape), pl.BlockSpec((owners, both // 2, width))),
        scratch_shapes=[pltpu.VMEM((3, table_rows + 8, width // 3), table.dtype)],
        name="settle",
    )(asked, counts, got, table)


def finish_kernel(every_ref, out_ref, *, scale):
    devices, rows, columns = every_ref.shape
    for d in range(devices):
        x, y, c = d // (2 * side), (d // 2) % side, d % 2
        left = (c * side + x) * columns
        out_ref[y * rows : (y + 1) * rows, left : left + columns] = (every_ref[d] * scale).astype(out_ref.dtype)


def finish(every, scale):
    _, rows, columns = every.shape
    return pl.pallas_call(
        functools.partial(finish_kernel, scale=scale),
        out_shape=jax.ShapeDtypeStruct((side * rows, 2 * side * columns), jnp.bfloat16),
        in_specs=[pl.BlockSpec(memory_space=pltpu.VMEM)],
        name="finish",
    )(every)


def swap_pairs():
    return [(d, d ^ 1) for d in range(2 * side * side)]


def planes():
    return [[2 * chip + c for chip in range(side * side)] for c in range(2)]


def local(
    cache_state,
    table_state,
    batch_idx,
    loss_grad,
    w_first,
    head,
    home,
    fetch_rows,
    fetch_counts,
    evict_rows,
    evict_from,
    evict_counts,
):
    group = lax.axis_size("shard")
    devices = lax.axis_size("dp")
    place = lax.axis_index("dp").astype(jnp.uint32)
    core = (place & 1).astype(jnp.int32)
    cache = cache_state[0, 0]
    table = table_state[0, 0]
    batch_t = batch_idx[0, 0].T
    loss = loss_grad[0]
    wanted = fetch_rows[0, 0]
    gone = evict_rows[0, 0]
    table_rows = table.shape[0]
    samples = loss.shape[1]
    mlp_width = w_first.shape[0]

    slots = lookup(home, wanted, gone, evict_counts[0], table_rows)
    asked = lax.all_to_all(slots, "shard", split_axis=0, concat_axis=0, tiled=True)

    cores = jnp.stack([1 - core, core])
    head_row = head[None]
    send, delta_a, inputs = forward_half(cores, group, cache, batch_t, None, None, loss, head_row, w_first)
    partner = lax.ppermute(send, "dp", swap_pairs())
    partner = pltpu.with_memory_space_constraint(partner, pltpu.VMEM)
    chip, delta_b = forward_half(cores, group, None, None, partner, inputs, loss, head_row, w_first)
    plane = side * side
    pieces = chip.reshape((plane,) + chip.shape[2:])
    pieces = lax.all_to_all(
        pieces, "dp", split_axis=0, concat_axis=0, axis_index_groups=planes(), tiled=True
    )
    sent = backward(cores, asked, evict_from[0, 0], cache, table, batch_t, delta_a, delta_b, w_first)
    sent = add_total(pltpu.with_memory_space_constraint(pieces, pltpu.VMEM), sent)
    got = lax.all_to_all(sent, "shard", split_axis=0, concat_axis=0, tiled=True)
    scale = 1.0 / math.sqrt(samples * group * devices)
    got = pltpu.with_memory_space_constraint(got, pltpu.VMEM)
    every = share_total(got, mlp_width // (group * side), devices)
    every = lax.all_to_all(every, "dp", split_axis=0, concat_axis=0, tiled=True)
    new_table, fetched = settle(asked, fetch_counts[0], got, table)
    grad_first = finish(pltpu.with_memory_space_constraint(every, pltpu.VMEM), scale)
    return (grad_first, new_table[None, None], fetched[None, None])


def solution(mesh):
    placed = (
        P("dp", "shard", None, None),
        P("dp", "shard", None, None),
        P("dp", "shard", None, None),
        P("dp", "shard", None),
        P(),
        P(),
        P("dp", None),
        P("dp", "shard", None, None),
        P("dp", "shard", None),
        P("dp", "shard", None, None),
        P("dp", "shard", None, None),
        P("dp", "shard", None),
    )

    return jax.shard_map(
        local,
        mesh=mesh,
        in_specs=placed,
        out_specs=(
            P("shard", None),
            P("dp", "shard", None, None),
            P("dp", "shard", None, None, None),
        ),
        check_vma=False,
    )
```

```python
import functools
import math

import jax
import jax.numpy as jnp
from jax import lax
from jax.experimental import pallas as pl
from jax.experimental.pallas import tpu as pltpu
from jax.sharding import PartitionSpec as P


beta_one = 0.9
beta_two = 0.999
learn_rate = 0.05
epsilon = 1e-08
bias_one = 1.0 - 0.9**10
bias_two = 1.0 - 0.999**10
NN = (((1,), (0,)), ((), ()))
NT = (((1,), (1,)), ((), ()))
TN = (((0,), (0,)), ((), ()))
side = 4


def full(shape):
    return pl.BlockSpec(shape, lambda j, o: tuple(0 for _ in shape))


def column(row):
    return jnp.transpose(jnp.broadcast_to(row, (8, row.shape[1])))[:, :1]


def onehot(batch_row, rows):
    shape = (rows, batch_row.shape[1])
    hit = lax.broadcasted_iota(jnp.int32, shape, 0) == batch_row
    return hit.astype(jnp.float32).astype(jnp.bfloat16)


def turn(outer, inner):
    return (3 * outer) ^ inner


def hidden(j, info, inputs, loss, head, w, delta_ref):
    width = delta_ref.shape[1]
    pre = lax.dot_general(w, inputs, TN, preferred_element_type=jnp.float32)
    sigma = jax.nn.sigmoid(pre)
    delta = (loss * column(head) * sigma * (1.0 + pre * (1.0 - sigma))).astype(jnp.bfloat16)
    for u in range(2):
        delta_ref[turn(j, u) ^ info[2]] = delta[u * width : (u + 1) * width]
    return lax.dot_general(inputs, delta, NT, preferred_element_type=jnp.float32)


def store_pieces(j, info, grad_ref, outs, plus_ref):
    owners, rows, columns = outs[0].shape[-3:]
    deep = 2 * side * rows
    for v in range(2):
        for o in range(2):
            y = turn(o, v) ^ info[3]
            for u in range(2):
                left = slice(u * columns, (u + 1) * columns)
                for z in range(owners):
                    even = grad_ref[pl.ds(pl.multiple_of(z * deep + y * rows, rows), rows), left]
                    odd = grad_ref[pl.ds(pl.multiple_of(z * deep + side * rows + y * rows, rows), rows), left]
                    if plus_ref is not None:
                        even += plus_ref[u, j, v, o, z]
                        odd += plus_ref[2 + v, o, u, j, z]
                    outs[u][j, v, o, z] = even
                    outs[2 + v][o, u, j, z] = odd


def first_kernel(
    info, cache_ref, batch_ref, loss_ref, head_a, head_b, w_a, w_b, grad_out, delta_ref, inputs_ref, grad_ref
):
    rows = cache_ref.shape[0]
    features = batch_ref.shape[0]
    embed = inputs_ref.shape[0] // features
    j = pl.program_id(0)

    @pl.when(j == 0)
    def _():
        looked = jnp.transpose(cache_ref[...]).astype(jnp.bfloat16)
        for f in range(features):
            pick = onehot(batch_ref[f : f + 1, :], rows)
            inputs_ref[f * embed : (f + 1) * embed, :] = lax.dot_general(
                looked, pick, NN, preferred_element_type=jnp.float32
            ).astype(jnp.bfloat16)

    head = jnp.concatenate([head_a[...], head_b[...]], 1)
    w = jnp.concatenate([w_a[...], w_b[...]], 1)
    grad_ref[...] = hidden(j, info, inputs_ref[...], loss_ref[...], head, w, delta_ref)
    store_pieces(j, info, grad_ref, [grad_out.at[i] for i in range(4)], None)


def second_kernel(
    info, plus_ref, inputs_ref, loss_ref, head_a, head_b, w_a, w_b, out_a, out_b, out_c, out_d, delta_ref, grad_ref
):
    j = pl.program_id(0)
    head = jnp.concatenate([head_a[...], head_b[...]], 1)
    w = jnp.concatenate([w_a[...], w_b[...]], 1)
    grad_ref[...] = hidden(j, info, inputs_ref[...], loss_ref[...], head, w, delta_ref)
    store_pieces(j, info, grad_ref, [out_a, out_b, out_c, out_d], plus_ref)


def forward_half(info, owners, cache, batch_t, partner, inputs, loss, head, w):
    samples = loss.shape[1]
    width = w.shape[0]
    half = width // 2
    block = half // side
    here = 0 if inputs is None else 1
    whole = pl.BlockSpec(memory_space=pltpu.VMEM)
    part = lambda u: lambda j, c: (0, side * c[here] + (turn(j, u) ^ c[2]))
    tail_specs = [full((1, samples))]
    tail_specs += [pl.BlockSpec((1, block), part(u)) for u in range(2)]
    tail_specs += [pl.BlockSpec((width, block), part(u)) for u in range(2)]
    piece = (2, 2, 2, owners, width // (owners * 2 * side), block)
    delta = jax.ShapeDtypeStruct((side, block, samples), jnp.bfloat16)
    scratch = [pltpu.VMEM((width, 2 * block), jnp.float32)]
    if inputs is None:
        rows = cache.shape[0]
        embed = cache.shape[1] // 3
        return pl.pallas_call(
            first_kernel,
            out_shape=(
                jax.ShapeDtypeStruct((4,) + piece, jnp.float32),
                delta,
                jax.ShapeDtypeStruct((width, samples), jnp.bfloat16),
            ),
            grid_spec=pltpu.PrefetchScalarGridSpec(
                num_scalar_prefetch=1,
                grid=(2,),
                in_specs=[pl.BlockSpec((rows, embed), lambda j, c: (0, 0)), full(batch_t.shape)] + tail_specs,
                out_specs=(whole, whole, whole),
                scratch_shapes=scratch,
            ),
            name="forward_first",
        )(info, cache, batch_t, loss, head, head, w, w)
    return pl.pallas_call(
        second_kernel,
        out_shape=tuple(jax.ShapeDtypeStruct(piece, jnp.float32) for _ in range(4)) + (delta,),
        grid_spec=pltpu.PrefetchScalarGridSpec(
            num_scalar_prefetch=1,
            grid=(2,),
            in_specs=[whole, whole] + tail_specs,
            out_specs=(whole,) * 5,
            scratch_shapes=scratch,
        ),
        name="forward_second",
    )(info, partner, inputs, loss, head, head, w, w)


def backward_kernel(
    info, leaving, cache_ref, ids_ref, batch_ref, delta_a, delta_b, w_a, w_b, sent_ref, acc_ref, upd_ref
):
    rows, width = cache_ref.shape
    embed = width // 3
    owners, capacity = leaving.shape
    step = pl.program_id(0)
    half = w_a.shape[1]
    back = lax.dot_general(w_a[...], delta_a[...].reshape(half, -1), NN, preferred_element_type=jnp.float32)
    back += lax.dot_general(w_b[...], delta_b[...].reshape(half, -1), NN, preferred_element_type=jnp.float32)
    total = None
    for k in range(w_a.shape[0] // embed):
        part = back[k * embed : (k + 1) * embed]
        high = part.astype(jnp.bfloat16)
        low = (part - high.astype(jnp.float32)).astype(jnp.bfloat16)
        pick = onehot(batch_ref[pl.ds(step * (w_a.shape[0] // embed) + k, 1), :], rows)
        add = lax.dot_general(jnp.concatenate([high, low], 0), pick, NT, preferred_element_type=jnp.float32)
        total = add if total is None else total + add

    @pl.when(step == 0)
    def _():
        acc_ref[...] = total
        sent_ref[:, 3 * capacity :, :] = ids_ref[...]

    @pl.when(step > 0)
    def _():
        acc_ref[...] += total

    @pl.when(step == pl.num_programs(0) - 1)
    def _():
        grads = jnp.transpose(acc_ref[:embed, :] + acc_ref[embed:, :])
        value = cache_ref[:, :embed]
        first = cache_ref[:, embed : 2 * embed]
        second = cache_ref[:, 2 * embed :]
        first = beta_one * first + (1.0 - beta_one) * grads
        second = beta_two * second + (1.0 - beta_two) * grads * grads
        upd_ref[:, :embed] = value - learn_rate * (first / bias_one) / (jnp.sqrt(second / bias_two) + epsilon)
        upd_ref[:, embed : 2 * embed] = first
        upd_ref[:, 2 * embed :] = second

        def evict(i, carry):
            for k in range(capacity):
                row = upd_ref[pl.ds(leaving[i, k], 1), :]
                for p in range(3):
                    at = p * capacity + k
                    sent_ref[i, at : at + 1, :] = row[:, p * embed : (p + 1) * embed]
            return carry

        lax.fori_loop(0, owners, evict, 0)


def backward(info, leaving, cache, ids, batch_t, delta_a, delta_b, w):
    rows, width3 = cache.shape
    embed = width3 // 3
    features, _ = batch_t.shape
    width = w.shape[0]
    half = width // 2
    steps = features // 2
    owners, capacity = leaving.shape
    fixed = lambda shape: pl.BlockSpec(shape, lambda j, c, e: tuple(0 for _ in shape))
    whole = pl.BlockSpec(memory_space=pltpu.VMEM)
    sent = (owners, 3 * capacity + ids.shape[1], embed)
    return pl.pallas_call(
        backward_kernel,
        out_shape=jax.ShapeDtypeStruct(sent, jnp.float32),
        grid_spec=pltpu.PrefetchScalarGridSpec(
            num_scalar_prefetch=2,
            grid=(steps,),
            in_specs=[
                fixed(cache.shape),
                fixed(ids.shape),
                fixed(batch_t.shape),
                whole,
                whole,
                pl.BlockSpec((2 * embed, half), lambda j, c, e: (j, c[0])),
                pl.BlockSpec((2 * embed, half), lambda j, c, e: (j, c[1])),
            ],
            out_specs=fixed(sent),
            scratch_shapes=[pltpu.VMEM((2 * embed, rows), jnp.float32), pltpu.VMEM((rows, width3), jnp.float32)],
        ),
        name="backward",
    )(info, leaving, cache, ids, batch_t, delta_a, delta_b, w, w)


def serve_kernel(asked_ref, table_ref, even_a, even_b, odd_a, odd_b, out_ref):
    owners, both = asked_ref.shape
    capacity = both // 2
    embed = out_ref.shape[2]
    rows = even_a.shape[1]

    def fetch(i, carry):
        for k in range(capacity):
            row = table_ref[pl.ds(asked_ref[i, k], 1), :]
            for p in range(3):
                at = p * capacity + k
                out_ref[i, at : at + 1, :] = row[:, p * embed : (p + 1) * embed]
        return carry

    lax.fori_loop(0, owners, fetch, 0)
    out_ref[:, 3 * capacity : 3 * capacity + rows, :] = even_a[...] + even_b[...]
    out_ref[:, 3 * capacity + rows :, :] = odd_a[...] + odd_b[...]


def serve(asked, table, even, odd):
    owners, both = asked.shape
    _, rows, embed = even[0].shape
    whole = pl.BlockSpec(memory_space=pltpu.VMEM)
    return pl.pallas_call(
        serve_kernel,
        out_shape=jax.ShapeDtypeStruct((owners, 3 * both // 2 + 2 * rows, embed), jnp.float32),
        in_specs=[pl.BlockSpec(memory_space=pltpu.SMEM), pl.BlockSpec(table.shape)] + [whole] * 4,
        name="serve",
    )(asked, table, *even, *odd)


def lookup_kernel(home_ref, wanted_ref, gone_ref, counts_ref, out_ref, *, table_rows):
    owners, capacity = wanted_ref.shape

    def look(i, carry):
        count = counts_ref[0, i]
        for k in range(capacity):
            out_ref[i, k] = home_ref[0, wanted_ref[i, k]] & (table_rows - 1)
            slot = home_ref[0, gone_ref[i, k]] & (table_rows - 1)
            out_ref[i, capacity + k] = jnp.where(k < count, slot, table_rows)
        return carry

    lax.fori_loop(0, owners, look, 0)


def lookup(home, wanted, gone, counts, table_rows):
    owners, capacity = wanted.shape
    scalar = pl.BlockSpec(memory_space=pltpu.SMEM)
    return pl.pallas_call(
        functools.partial(lookup_kernel, table_rows=table_rows),
        out_shape=jax.ShapeDtypeStruct((owners, 2 * capacity), jnp.int32),
        in_specs=[scalar] * 4,
        out_specs=scalar,
        name="lookup",
    )(home, wanted, gone, counts)


def share_kernel(got_ref, out_ref):
    rows = out_ref.shape[1]
    last = pl.ds(got_ref.shape[1] - rows, rows)
    total = got_ref[0, last]
    for i in range(1, got_ref.shape[0]):
        total += got_ref[i, last]
    for d in range(out_ref.shape[0]):
        out_ref[d] = total


def share_total(got, rows, devices):
    return pl.pallas_call(
        share_kernel,
        out_shape=jax.ShapeDtypeStruct((devices, rows, got.shape[2]), got.dtype),
        in_specs=[pl.BlockSpec(memory_space=pltpu.VMEM)],
        name="share_total",
    )(got)


def settle_kernel(asked_ref, got_ref, table_ref, new_ref, rows_ref):
    owners, both = asked_ref.shape
    capacity = both // 2
    embed = got_ref.shape[2]
    table_rows = table_ref.shape[0]
    for p in range(3):
        rows_ref[p, :table_rows] = table_ref[:, p * embed : (p + 1) * embed]

    def place(i, carry):
        for k in range(capacity):
            slot = asked_ref[i, capacity + k]
            for p in range(3):
                at = p * capacity + k
                rows_ref[p, pl.ds(slot, 1), :] = got_ref[i, at : at + 1, :]
        return carry

    lax.fori_loop(0, owners, place, 0)
    for p in range(3):
        new_ref[:, p * embed : (p + 1) * embed] = rows_ref[p, :table_rows]


def settle(asked, got, table):
    table_rows, width = table.shape
    return pl.pallas_call(
        settle_kernel,
        out_shape=jax.ShapeDtypeStruct(table.shape, table.dtype),
        in_specs=[
            pl.BlockSpec(memory_space=pltpu.SMEM),
            pl.BlockSpec(memory_space=pltpu.VMEM),
            pl.BlockSpec(table.shape),
        ],
        out_specs=pl.BlockSpec(table.shape),
        scratch_shapes=[pltpu.VMEM((3, table_rows + 8, width // 3), table.dtype)],
        name="settle",
    )(asked, got, table)


def mask_kernel(counts_ref, got_ref, fetched_ref):
    owners, capacity, width = fetched_ref.shape
    embed = width // 3
    for i in range(owners):
        live = lax.broadcasted_iota(jnp.int32, (capacity, embed), 0) < counts_ref[0, i]
        for p in range(3):
            block = got_ref[i, p * capacity : (p + 1) * capacity, :]
            fetched_ref[i, :, p * embed : (p + 1) * embed] = jnp.where(live, block, 0.0)


def mask_rows(counts, got, capacity):
    return pl.pallas_call(
        mask_kernel,
        out_shape=jax.ShapeDtypeStruct((got.shape[0], capacity, 3 * got.shape[2]), got.dtype),
        in_specs=[pl.BlockSpec(memory_space=pltpu.SMEM), pl.BlockSpec(memory_space=pltpu.VMEM)],
        name="mask_rows",
    )(counts, got)


def finish_kernel(every_ref, out_ref, *, scale):
    _, both, columns = every_ref.shape
    rows = both // 2
    for x in range(side):
        for c in range(2):
            left = (c * side + x) * columns
            for k in range(2):
                for y in range(0, side, 2):
                    pair = [every_ref[(x * side + y + i) * 2 + c, k * rows : (k + 1) * rows] for i in range(2)]
                    top = (k * side + y) * rows
                    out_ref[top : top + both, left : left + columns] = (
                        jnp.concatenate(pair, 0) * scale
                    ).astype(out_ref.dtype)


def finish(every, scale):
    _, rows, columns = every.shape
    return pl.pallas_call(
        functools.partial(finish_kernel, scale=scale),
        out_shape=jax.ShapeDtypeStruct((side * rows, 2 * side * columns), jnp.bfloat16),
        in_specs=[pl.BlockSpec(memory_space=pltpu.VMEM)],
        name="finish",
    )(every)


def pairs(core, x, y):
    bits = (x * side + y) * 2 + core
    return [(d, d ^ bits) for d in range(2 * side * side)]


def send_to(a, x, y):
    return lax.ppermute(a, "dp", pairs(0, x, y))


def on_chip(a):
    return pltpu.with_memory_space_constraint(a, pltpu.VMEM)


def local(
    cache_state,
    table_state,
    batch_idx,
    loss_grad,
    w_first,
    head,
    home,
    fetch_rows,
    fetch_counts,
    evict_rows,
    evict_from,
    evict_counts,
):
    group = lax.axis_size("shard")
    devices = lax.axis_size("dp")
    place = lax.axis_index("dp").astype(jnp.uint32)
    core = (place & 1).astype(jnp.int32)
    cache = cache_state[0, 0]
    table = table_state[0, 0]
    batch_t = batch_idx[0, 0].T
    loss = loss_grad[0]
    wanted = fetch_rows[0, 0]
    gone = evict_rows[0, 0]
    table_rows = table.shape[0]
    capacity = wanted.shape[1]
    samples = loss.shape[1]
    mlp_width = w_first.shape[0]

    info = jnp.stack([1 - core, core, (place >> 3).astype(jnp.int32), ((place >> 1) & 3).astype(jnp.int32)])
    head_row = head[None]
    send, delta_a, inputs = forward_half(info, group, cache, batch_t, None, None, loss, head_row, w_first)
    partner = on_chip(lax.ppermute(send, "dp", pairs(1, 0, 0)))
    slots = lookup(home, wanted, gone, evict_counts[0], table_rows)
    lanes = cache.shape[1] // 3
    ids = jnp.pad(slots.astype(jnp.float32), ((0, 0), (0, lanes - slots.shape[1])))
    ids = jnp.broadcast_to(ids[:, None, :], (group, 8, lanes))
    even, even_out, odd, odd_out, delta_b = forward_half(
        info, group, None, None, partner, inputs, loss, head_row, w_first
    )
    even += send_to(even_out, 1, 0)
    odd += send_to(odd_out, 0, 1)
    sent = backward(info, evict_from[0, 0], cache, ids, batch_t, delta_a, delta_b, w_first)
    even = even[0] + send_to(even[1], 3, 0)
    odd = odd[0] + send_to(odd[1], 0, 3)
    got = lax.all_to_all(sent, "shard", split_axis=0, concat_axis=0, tiled=True)
    even = even[0] + send_to(even[1], 0, 1)
    odd = odd[0] + send_to(odd[1], 1, 0)
    even = (even[0], on_chip(send_to(even[1], 0, 3)))
    odd = (odd[0], on_chip(send_to(odd[1], 3, 0)))
    asked = got[:, 3 * capacity, : 2 * capacity].astype(jnp.int32)
    served = serve(asked, table, even, odd)
    came = on_chip(lax.all_to_all(served, "shard", split_axis=0, concat_axis=0, tiled=True))
    new_table = settle(asked, on_chip(got), table)
    scale = 1.0 / math.sqrt(samples * group * devices)
    every = share_total(came, mlp_width // (group * side), devices)
    every = on_chip(lax.all_to_all(every, "dp", split_axis=0, concat_axis=0, tiled=True))
    fetched = mask_rows(fetch_counts[0], came, capacity)
    grad_first = finish(every, scale)
    return (grad_first, new_table[None, None], fetched[None, None])


def solution(mesh):
    placed = (
        P("dp", "shard", None, None),
        P("dp", "shard", None, None),
        P("dp", "shard", None, None),
        P("dp", "shard", None),
        P(),
        P(),
        P("dp", None),
        P("dp", "shard", None, None),
        P("dp", "shard", None),
        P("dp", "shard", None, None),
        P("dp", "shard", None, None),
        P("dp", "shard", None),
    )

    return jax.shard_map(
        local,
        mesh=mesh,
        in_specs=placed,
        out_specs=(
            P("shard", None),
            P("dp", "shard", None, None),
            P("dp", "shard", None, None, None),
        ),
        check_vma=False,
    )
```

```python
import functools
import math

import jax
import jax.numpy as jnp
from jax import lax
from jax.experimental import pallas as pl
from jax.experimental.pallas import tpu as pltpu
from jax.sharding import PartitionSpec as P


beta_one = 0.9
beta_two = 0.999
learn_rate = 0.05
epsilon = 1e-08
bias_one = 1.0 - 0.9**10
bias_two = 1.0 - 0.999**10
NN = (((1,), (0,)), ((), ()))
NT = (((1,), (1,)), ((), ()))
TN = (((0,), (0,)), ((), ()))
side = 4


def full(shape):
    return pl.BlockSpec(shape, lambda j, o: tuple(0 for _ in shape))


def column(row):
    return jnp.transpose(jnp.broadcast_to(row, (8, row.shape[1])))[:, :1]


def onehot(batch_row, rows):
    shape = (rows, batch_row.shape[1])
    hit = lax.broadcasted_iota(jnp.int32, shape, 0) == batch_row
    return hit.astype(jnp.float32).astype(jnp.bfloat16)


def turn(outer, inner):
    return (3 * outer) ^ inner


def hidden(j, info, inputs, loss, head, w, delta_ref):
    pre = lax.dot_general(w, inputs, TN, preferred_element_type=jnp.float32)
    sigma = jax.nn.sigmoid(pre)
    delta = (loss * column(head) * sigma * (1.0 + pre * (1.0 - sigma))).astype(jnp.bfloat16)
    for u in range(2):
        delta_ref[(turn(j, u) ^ info[2]) & 1] = delta[u * (delta.shape[0] // 2) : (u + 1) * (delta.shape[0] // 2)]
    return lax.dot_general(inputs, delta, NT, preferred_element_type=jnp.float32)


def store_pieces(j, info, grad_ref, outs, plus_ref):
    owners, rows, columns = outs[0].shape[-3:]
    deep = 2 * side * rows
    for v in range(2):
        for o in range(2):
            y = turn(o, v) ^ info[3]
            for u in range(2):
                left = slice(u * columns, (u + 1) * columns)
                for z in range(owners):
                    even = grad_ref[pl.ds(pl.multiple_of(z * deep + y * rows, rows), rows), left]
                    odd = grad_ref[pl.ds(pl.multiple_of(z * deep + side * rows + y * rows, rows), rows), left]
                    if plus_ref is not None:
                        even += plus_ref[u, j, v, o, z]
                        odd += plus_ref[2 + v, j, o, u, z]
                    outs[u][0, v, o, z] = even
                    if plus_ref is None:
                        outs[2 + v][0, o, u, z] = odd
                    else:
                        outs[2 + v][o, u, 0, z] = odd


def gather(cache_ref, batch_ref, inputs_ref):
    rows = cache_ref.shape[0]
    features = batch_ref.shape[0]
    embed = inputs_ref.shape[0] // features

    @pl.when(pl.program_id(0) == 0)
    def _():
        looked = jnp.transpose(cache_ref[...]).astype(jnp.bfloat16)
        for f in range(features):
            pick = onehot(batch_ref[f : f + 1, :], rows)
            inputs_ref[f * embed : (f + 1) * embed, :] = lax.dot_general(
                looked, pick, NN, preferred_element_type=jnp.float32
            ).astype(jnp.bfloat16)


def first_kernel(
    info, cache_ref, batch_ref, loss_ref, head_a, head_b, w_a, w_b, grad_out, delta_ref, inputs_ref, grad_ref
):
    j = pl.program_id(0)
    gather(cache_ref, batch_ref, inputs_ref)
    head = jnp.concatenate([head_a[...], head_b[...]], 1)
    w = jnp.concatenate([w_a[...], w_b[...]], 1)
    grad_ref[...] = hidden(j, info, inputs_ref[...], loss_ref[...], head, w, delta_ref)
    store_pieces(j, info, grad_ref, [grad_out.at[i] for i in range(4)], None)


def second_kernel(
    info,
    plus_ref,
    cache_ref,
    batch_ref,
    loss_ref,
    head_a,
    head_b,
    w_a,
    w_b,
    out_a,
    out_b,
    out_c,
    out_d,
    delta_ref,
    inputs_ref,
    grad_ref,
):
    j = pl.program_id(0)
    gather(cache_ref, batch_ref, inputs_ref)
    head = jnp.concatenate([head_a[...], head_b[...]], 1)
    w = jnp.concatenate([w_a[...], w_b[...]], 1)
    grad_ref[...] = hidden(j, info, inputs_ref[...], loss_ref[...], head, w, delta_ref)
    store_pieces(j, info, grad_ref, [out_a, out_b, out_c, out_d], plus_ref)


def forward_half(info, owners, cache, batch_t, partner, loss, head, w):
    samples = loss.shape[1]
    width = w.shape[0]
    half = width // 2
    block = half // side
    here = 0 if partner is None else 1
    rows = cache.shape[0]
    embed = cache.shape[1] // 3
    part = lambda u: lambda j, c: (0, side * c[here] + (turn(j, u) ^ c[2]))
    specs = [pl.BlockSpec((rows, embed), lambda j, c: (0, 0)), full(batch_t.shape), full((1, samples))]
    specs += [pl.BlockSpec((1, block), part(u)) for u in range(2)]
    specs += [pl.BlockSpec((width, block), part(u)) for u in range(2)]
    piece = (2, 2, 2, owners, width // (owners * 2 * side), block)
    delta = jax.ShapeDtypeStruct((side, block, samples), jnp.bfloat16)
    delta_spec = pl.BlockSpec((2, block, samples), lambda j, c: (j ^ (c[2] >> 1), 0, 0))
    scratch = [pltpu.VMEM((width, samples), jnp.bfloat16), pltpu.VMEM((width, 2 * block), jnp.float32)]
    if partner is None:
        return pl.pallas_call(
            first_kernel,
            out_shape=(jax.ShapeDtypeStruct((4,) + piece, jnp.float32), delta),
            grid_spec=pltpu.PrefetchScalarGridSpec(
                num_scalar_prefetch=1,
                grid=(2,),
                in_specs=specs,
                out_specs=(pl.BlockSpec((4, 1) + piece[1:], lambda j, c: (0, j, 0, 0, 0, 0, 0)), delta_spec),
                scratch_shapes=scratch,
            ),
            name="forward_first",
        )(info, cache, batch_t, loss, head, head, w, w)
    even_spec = pl.BlockSpec((1,) + piece[1:], lambda j, c: (j, 0, 0, 0, 0, 0))
    odd_spec = pl.BlockSpec((2, 2, 1) + piece[3:], lambda j, c: (0, 0, j, 0, 0, 0))
    return pl.pallas_call(
        second_kernel,
        out_shape=tuple(jax.ShapeDtypeStruct(piece, jnp.float32) for _ in range(4)) + (delta,),
        grid_spec=pltpu.PrefetchScalarGridSpec(
            num_scalar_prefetch=1,
            grid=(2,),
            in_specs=[pl.BlockSpec(memory_space=pltpu.VMEM)] + specs,
            out_specs=(even_spec, even_spec, odd_spec, odd_spec, delta_spec),
            scratch_shapes=scratch,
        ),
        name="forward_second",
    )(info, partner, cache, batch_t, loss, head, head, w, w)


def backward_kernel(
    info, leaving, cache_ref, ids_ref, batch_ref, delta_a, delta_b, w_a, w_b, sent_ref, acc_ref, upd_ref
):
    rows, width = cache_ref.shape
    embed = width // 3
    owners, capacity = leaving.shape
    step = pl.program_id(0)
    half = w_a.shape[1]
    back = lax.dot_general(w_a[...], delta_a[...].reshape(half, -1), NN, preferred_element_type=jnp.float32)
    back += lax.dot_general(w_b[...], delta_b[...].reshape(half, -1), NN, preferred_element_type=jnp.float32)
    total = None
    for k in range(w_a.shape[0] // embed):
        part = back[k * embed : (k + 1) * embed]
        high = part.astype(jnp.bfloat16)
        low = (part - high.astype(jnp.float32)).astype(jnp.bfloat16)
        pick = onehot(batch_ref[pl.ds(step * (w_a.shape[0] // embed) + k, 1), :], rows)
        add = lax.dot_general(jnp.concatenate([high, low], 0), pick, NT, preferred_element_type=jnp.float32)
        total = add if total is None else total + add

    @pl.when(step == 0)
    def _():
        acc_ref[...] = total
        sent_ref[:, 3 * capacity :, :] = ids_ref[...]

    @pl.when(step > 0)
    def _():
        acc_ref[...] += total

    @pl.when(step == pl.num_programs(0) - 1)
    def _():
        grads = jnp.transpose(acc_ref[:embed, :] + acc_ref[embed:, :])
        value = cache_ref[:, :embed]
        first = cache_ref[:, embed : 2 * embed]
        second = cache_ref[:, 2 * embed :]
        first = beta_one * first + (1.0 - beta_one) * grads
        second = beta_two * second + (1.0 - beta_two) * grads * grads
        upd_ref[:, :embed] = value - learn_rate * (first / bias_one) / (jnp.sqrt(second / bias_two) + epsilon)
        upd_ref[:, embed : 2 * embed] = first
        upd_ref[:, 2 * embed :] = second

        def evict(i, carry):
            for k in range(capacity):
                row = upd_ref[pl.ds(leaving[i, k], 1), :]
                for p in range(3):
                    at = p * capacity + k
                    sent_ref[i, at : at + 1, :] = row[:, p * embed : (p + 1) * embed]
            return carry

        lax.fori_loop(0, owners, evict, 0)


def backward(info, leaving, cache, ids, batch_t, delta_a, delta_b, w):
    rows, width3 = cache.shape
    embed = width3 // 3
    features, _ = batch_t.shape
    width = w.shape[0]
    half = width // 2
    steps = features // 2
    owners, capacity = leaving.shape
    fixed = lambda shape: pl.BlockSpec(shape, lambda j, c, e: tuple(0 for _ in shape))
    whole = pl.BlockSpec(memory_space=pltpu.VMEM)
    sent = (owners, 3 * capacity + ids.shape[1], embed)
    return pl.pallas_call(
        backward_kernel,
        out_shape=jax.ShapeDtypeStruct(sent, jnp.float32),
        grid_spec=pltpu.PrefetchScalarGridSpec(
            num_scalar_prefetch=2,
            grid=(steps,),
            in_specs=[
                fixed(cache.shape),
                fixed(ids.shape),
                fixed(batch_t.shape),
                whole,
                whole,
                pl.BlockSpec((2 * embed, half), lambda j, c, e: (j, c[0])),
                pl.BlockSpec((2 * embed, half), lambda j, c, e: (j, c[1])),
            ],
            out_specs=fixed(sent),
            scratch_shapes=[pltpu.VMEM((2 * embed, rows), jnp.float32), pltpu.VMEM((rows, width3), jnp.float32)],
        ),
        name="backward",
    )(info, leaving, cache, ids, batch_t, delta_a, delta_b, w, w)


def serve_kernel(asked_ref, table_ref, even_a, even_b, odd_a, odd_b, out_ref):
    owners, both = asked_ref.shape
    capacity = both // 2
    embed = out_ref.shape[2]
    rows = even_a.shape[1]

    def fetch(i, carry):
        for k in range(capacity):
            row = table_ref[pl.ds(asked_ref[i, k], 1), :]
            for p in range(3):
                at = p * capacity + k
                out_ref[i, at : at + 1, :] = row[:, p * embed : (p + 1) * embed]
        return carry

    lax.fori_loop(0, owners, fetch, 0)
    out_ref[:, 3 * capacity : 3 * capacity + rows, :] = even_a[...] + even_b[...]
    out_ref[:, 3 * capacity + rows :, :] = odd_a[...] + odd_b[...]


def serve(asked, table, even, odd):
    owners, both = asked.shape
    _, rows, embed = even[0].shape
    whole = pl.BlockSpec(memory_space=pltpu.VMEM)
    return pl.pallas_call(
        serve_kernel,
        out_shape=jax.ShapeDtypeStruct((owners, 3 * both // 2 + 2 * rows, embed), jnp.float32),
        in_specs=[pl.BlockSpec(memory_space=pltpu.SMEM), pl.BlockSpec(table.shape)] + [whole] * 4,
        name="serve",
    )(asked, table, *even, *odd)


def lookup_kernel(home_ref, wanted_ref, gone_ref, counts_ref, out_ref, *, table_rows):
    owners, capacity = wanted_ref.shape

    def look(i, carry):
        count = counts_ref[0, i]
        for k in range(capacity):
            out_ref[i, k] = home_ref[0, wanted_ref[i, k]] & (table_rows - 1)
            slot = home_ref[0, gone_ref[i, k]] & (table_rows - 1)
            out_ref[i, capacity + k] = jnp.where(k < count, slot, table_rows)
        return carry

    lax.fori_loop(0, owners, look, 0)


def lookup(home, wanted, gone, counts, table_rows):
    owners, capacity = wanted.shape
    scalar = pl.BlockSpec(memory_space=pltpu.SMEM)
    return pl.pallas_call(
        functools.partial(lookup_kernel, table_rows=table_rows),
        out_shape=jax.ShapeDtypeStruct((owners, 2 * capacity), jnp.int32),
        in_specs=[scalar] * 4,
        out_specs=scalar,
        name="lookup",
    )(home, wanted, gone, counts)


def share_kernel(got_ref, out_ref):
    rows = out_ref.shape[1]
    last = pl.ds(got_ref.shape[1] - rows, rows)
    total = got_ref[0, last]
    for i in range(1, got_ref.shape[0]):
        total += got_ref[i, last]
    for d in range(out_ref.shape[0]):
        out_ref[d] = total


def share_total(got, rows, devices):
    return pl.pallas_call(
        share_kernel,
        out_shape=jax.ShapeDtypeStruct((devices, rows, got.shape[2]), got.dtype),
        in_specs=[pl.BlockSpec(memory_space=pltpu.VMEM)],
        name="share_total",
    )(got)


def settle_kernel(asked_ref, got_ref, table_ref, new_ref, rows_ref):
    owners, both = asked_ref.shape
    capacity = both // 2
    embed = got_ref.shape[2]
    table_rows = table_ref.shape[0]
    for p in range(3):
        rows_ref[p, :table_rows] = table_ref[:, p * embed : (p + 1) * embed]

    def place(i, carry):
        for k in range(capacity):
            slot = asked_ref[i, capacity + k]
            for p in range(3):
                at = p * capacity + k
                rows_ref[p, pl.ds(slot, 1), :] = got_ref[i, at : at + 1, :]
        return carry

    lax.fori_loop(0, owners, place, 0)
    for p in range(3):
        new_ref[:, p * embed : (p + 1) * embed] = rows_ref[p, :table_rows]


def settle(asked, got, table):
    table_rows, width = table.shape
    return pl.pallas_call(
        settle_kernel,
        out_shape=jax.ShapeDtypeStruct(table.shape, table.dtype),
        in_specs=[
            pl.BlockSpec(memory_space=pltpu.SMEM),
            pl.BlockSpec(memory_space=pltpu.VMEM),
            pl.BlockSpec(table.shape),
        ],
        out_specs=pl.BlockSpec(table.shape),
        scratch_shapes=[pltpu.VMEM((3, table_rows + 8, width // 3), table.dtype)],
        name="settle",
    )(asked, got, table)


def mask_kernel(counts_ref, got_ref, fetched_ref):
    owners, capacity, width = fetched_ref.shape
    embed = width // 3
    for i in range(owners):
        live = lax.broadcasted_iota(jnp.int32, (capacity, embed), 0) < counts_ref[0, i]
        for p in range(3):
            block = got_ref[i, p * capacity : (p + 1) * capacity, :]
            fetched_ref[i, :, p * embed : (p + 1) * embed] = jnp.where(live, block, 0.0)


def mask_rows(counts, got, capacity):
    return pl.pallas_call(
        mask_kernel,
        out_shape=jax.ShapeDtypeStruct((got.shape[0], capacity, 3 * got.shape[2]), got.dtype),
        in_specs=[pl.BlockSpec(memory_space=pltpu.SMEM), pl.BlockSpec(memory_space=pltpu.VMEM)],
        name="mask_rows",
    )(counts, got)


def finish_kernel(every_ref, out_ref, *, scale):
    _, both, columns = every_ref.shape
    rows = both // 2
    for x in range(side):
        for c in range(2):
            left = (c * side + x) * columns
            for k in range(2):
                for y in range(0, side, 2):
                    pair = [every_ref[(x * side + y + i) * 2 + c, k * rows : (k + 1) * rows] for i in range(2)]
                    top = (k * side + y) * rows
                    out_ref[top : top + both, left : left + columns] = (
                        jnp.concatenate(pair, 0) * scale
                    ).astype(out_ref.dtype)


def finish(every, scale):
    _, rows, columns = every.shape
    return pl.pallas_call(
        functools.partial(finish_kernel, scale=scale),
        out_shape=jax.ShapeDtypeStruct((side * rows, 2 * side * columns), jnp.bfloat16),
        in_specs=[pl.BlockSpec(memory_space=pltpu.VMEM)],
        name="finish",
    )(every)


def pairs(core, x, y):
    bits = (x * side + y) * 2 + core
    return [(d, d ^ bits) for d in range(2 * side * side)]


def send_to(a, x, y):
    return lax.ppermute(a, "dp", pairs(0, x, y))


def on_chip(a):
    return pltpu.with_memory_space_constraint(a, pltpu.VMEM)


def local(
    cache_state,
    table_state,
    batch_idx,
    loss_grad,
    w_first,
    head,
    home,
    fetch_rows,
    fetch_counts,
    evict_rows,
    evict_from,
    evict_counts,
):
    group = lax.axis_size("shard")
    devices = lax.axis_size("dp")
    place = lax.axis_index("dp").astype(jnp.uint32)
    core = (place & 1).astype(jnp.int32)
    cache = cache_state[0, 0]
    table = table_state[0, 0]
    batch_t = batch_idx[0, 0].T
    loss = loss_grad[0]
    wanted = fetch_rows[0, 0]
    gone = evict_rows[0, 0]
    table_rows = table.shape[0]
    capacity = wanted.shape[1]
    samples = loss.shape[1]
    mlp_width = w_first.shape[0]

    info = jnp.stack([1 - core, core, (place >> 3).astype(jnp.int32), ((place >> 1) & 3).astype(jnp.int32)])
    head_row = head[None]
    send, delta_a = forward_half(info, group, cache, batch_t, None, loss, head_row, w_first)
    partner = on_chip(lax.ppermute(send, "dp", pairs(1, 0, 0)))
    slots = lookup(home, wanted, gone, evict_counts[0], table_rows)
    lanes = cache.shape[1] // 3
    ids = jnp.pad(slots.astype(jnp.float32), ((0, 0), (0, lanes - slots.shape[1])))
    ids = jnp.broadcast_to(ids[:, None, :], (group, 8, lanes))
    even, even_out, odd, odd_out, delta_b = forward_half(info, group, cache, batch_t, partner, loss, head_row, w_first)
    even += send_to(even_out, 1, 0)
    odd += send_to(odd_out, 0, 1)
    sent = backward(
        info, evict_from[0, 0], cache, ids, batch_t, on_chip(delta_a), on_chip(delta_b), w_first
    )
    even = even[0] + send_to(even[1], 3, 0)
    odd = odd[0] + send_to(odd[1], 0, 3)
    got = lax.all_to_all(sent, "shard", split_axis=0, concat_axis=0, tiled=True)
    even = even[0] + send_to(even[1], 0, 1)
    odd = odd[0] + send_to(odd[1], 1, 0)
    even = (even[0], on_chip(send_to(even[1], 0, 3)))
    odd = (odd[0], on_chip(send_to(odd[1], 3, 0)))
    asked = got[:, 3 * capacity, : 2 * capacity].astype(jnp.int32)
    served = serve(asked, table, even, odd)
    came = on_chip(lax.all_to_all(served, "shard", split_axis=0, concat_axis=0, tiled=True))
    new_table = settle(asked, on_chip(got), table)
    scale = 1.0 / math.sqrt(samples * group * devices)
    every = share_total(came, mlp_width // (group * side), devices)
    every = on_chip(lax.all_to_all(every, "dp", split_axis=0, concat_axis=0, tiled=True))
    fetched = mask_rows(fetch_counts[0], came, capacity)
    grad_first = finish(every, scale)
    return (grad_first, new_table[None, None], fetched[None, None])


def solution(mesh):
    placed = (
        P("dp", "shard", None, None),
        P("dp", "shard", None, None),
        P("dp", "shard", None, None),
        P("dp", "shard", None),
        P(),
        P(),
        P("dp", None),
        P("dp", "shard", None, None),
        P("dp", "shard", None),
        P("dp", "shard", None, None),
        P("dp", "shard", None, None),
        P("dp", "shard", None),
    )

    return jax.shard_map(
        local,
        mesh=mesh,
        in_specs=placed,
        out_specs=(
            P("shard", None),
            P("dp", "shard", None, None),
            P("dp", "shard", None, None, None),
        ),
        check_vma=False,
    )
```

```python
import functools
import math

import jax
import jax.numpy as jnp
from jax import lax
from jax.experimental import pallas as pl
from jax.experimental.pallas import tpu as pltpu
from jax.sharding import PartitionSpec as P


beta_one = 0.9
beta_two = 0.999
learn_rate = 0.05
epsilon = 1e-08
bias_one = 1.0 - 0.9**10
bias_two = 1.0 - 0.999**10
NN = (((1,), (0,)), ((), ()))
NT = (((1,), (1,)), ((), ()))
TN = (((0,), (0,)), ((), ()))
side = 4


def full(shape):
    return pl.BlockSpec(shape, lambda j, o: tuple(0 for _ in shape))


def column(row):
    return jnp.transpose(jnp.broadcast_to(row, (8, row.shape[1])))[:, :1]


def onehot(batch_row, rows):
    shape = (rows, batch_row.shape[1])
    hit = lax.broadcasted_iota(jnp.int32, shape, 0) == batch_row
    return hit.astype(jnp.float32).astype(jnp.bfloat16)


def turn(outer, inner):
    return (3 * outer) ^ inner


def hidden(j, info, inputs, loss, head, w, delta_ref):
    pre = lax.dot_general(w, inputs, TN, preferred_element_type=jnp.float32)
    sigma = jax.nn.sigmoid(pre)
    delta = (loss * column(head) * sigma * (1.0 + pre * (1.0 - sigma))).astype(jnp.bfloat16)
    for u in range(2):
        delta_ref[(turn(j, u) ^ info[2]) & 1] = delta[u * (delta.shape[0] // 2) : (u + 1) * (delta.shape[0] // 2)]
    return lax.dot_general(inputs, delta, NT, preferred_element_type=jnp.float32)


def store_pieces(j, info, grad_ref, outs, plus_ref):
    owners, rows, columns = outs[0].shape[-3:]
    deep = 2 * side * rows
    for v in range(2):
        for o in range(2):
            y = turn(o, v) ^ info[3]
            for u in range(2):
                left = slice(u * columns, (u + 1) * columns)
                for z in range(owners):
                    even = grad_ref[pl.ds(pl.multiple_of(z * deep + y * rows, rows), rows), left]
                    odd = grad_ref[pl.ds(pl.multiple_of(z * deep + side * rows + y * rows, rows), rows), left]
                    if plus_ref is not None:
                        even += plus_ref[u, j, v, o, z]
                        odd += plus_ref[2 + v, j, o, u, z]
                    if plus_ref is None:
                        outs[u][0, v, o, z] = even
                        outs[2 + v][0, o, u, z] = odd
                    else:
                        outs[u][v, 0, o, z] = even
                        outs[2 + v][u, 0, o, z] = odd


def gather(cache_ref, batch_ref, inputs_ref):
    rows = cache_ref.shape[0]
    features = batch_ref.shape[0]
    embed = inputs_ref.shape[0] // features

    @pl.when(pl.program_id(0) == 0)
    def _():
        looked = jnp.transpose(cache_ref[...]).astype(jnp.bfloat16)
        for f in range(features):
            pick = onehot(batch_ref[f : f + 1, :], rows)
            inputs_ref[f * embed : (f + 1) * embed, :] = lax.dot_general(
                looked, pick, NN, preferred_element_type=jnp.float32
            ).astype(jnp.bfloat16)


def first_kernel(
    info, cache_ref, batch_ref, loss_ref, head_a, head_b, w_a, w_b, grad_out, delta_ref, inputs_ref, grad_ref
):
    j = pl.program_id(0)
    gather(cache_ref, batch_ref, inputs_ref)
    head = jnp.concatenate([head_a[...], head_b[...]], 1)
    w = jnp.concatenate([w_a[...], w_b[...]], 1)
    grad_ref[...] = hidden(j, info, inputs_ref[...], loss_ref[...], head, w, delta_ref)
    store_pieces(j, info, grad_ref, [grad_out.at[i] for i in range(4)], None)


def second_kernel(
    info,
    plus_ref,
    cache_ref,
    batch_ref,
    loss_ref,
    head_a,
    head_b,
    w_a,
    w_b,
    out_a,
    out_b,
    out_c,
    out_d,
    delta_ref,
    inputs_ref,
    grad_ref,
):
    j = pl.program_id(0)
    gather(cache_ref, batch_ref, inputs_ref)
    head = jnp.concatenate([head_a[...], head_b[...]], 1)
    w = jnp.concatenate([w_a[...], w_b[...]], 1)
    grad_ref[...] = hidden(j, info, inputs_ref[...], loss_ref[...], head, w, delta_ref)
    store_pieces(j, info, grad_ref, [out_a, out_b, out_c, out_d], plus_ref)


def forward_half(info, owners, cache, batch_t, partner, loss, head, w):
    samples = loss.shape[1]
    width = w.shape[0]
    half = width // 2
    block = half // side
    here = 0 if partner is None else 1
    rows = cache.shape[0]
    embed = cache.shape[1] // 3
    part = lambda u: lambda j, c: (0, side * c[here] + (turn(j, u) ^ c[2]))
    specs = [pl.BlockSpec((rows, embed), lambda j, c: (0, 0)), full(batch_t.shape), full((1, samples))]
    specs += [pl.BlockSpec((1, block), part(u)) for u in range(2)]
    specs += [pl.BlockSpec((width, block), part(u)) for u in range(2)]
    piece = (2, 2, 2, owners, width // (owners * 2 * side), block)
    delta = jax.ShapeDtypeStruct((side, block, samples), jnp.bfloat16)
    delta_spec = pl.BlockSpec((2, block, samples), lambda j, c: (j ^ (c[2] >> 1), 0, 0))
    scratch = [pltpu.VMEM((width, samples), jnp.bfloat16), pltpu.VMEM((width, 2 * block), jnp.float32)]
    if partner is None:
        return pl.pallas_call(
            first_kernel,
            out_shape=(jax.ShapeDtypeStruct((4,) + piece, jnp.float32), delta),
            grid_spec=pltpu.PrefetchScalarGridSpec(
                num_scalar_prefetch=1,
                grid=(2,),
                in_specs=specs,
                out_specs=(pl.BlockSpec((4, 1) + piece[1:], lambda j, c: (0, j, 0, 0, 0, 0, 0)), delta_spec),
                scratch_shapes=scratch,
            ),
            name="forward_first",
        )(info, cache, batch_t, loss, head, head, w, w)
    out_spec = pl.BlockSpec((2, 1, 2) + piece[3:], lambda j, c: (0, j, 0, 0, 0, 0))
    return pl.pallas_call(
        second_kernel,
        out_shape=tuple(jax.ShapeDtypeStruct(piece, jnp.float32) for _ in range(4)) + (delta,),
        grid_spec=pltpu.PrefetchScalarGridSpec(
            num_scalar_prefetch=1,
            grid=(2,),
            in_specs=[pl.BlockSpec(memory_space=pltpu.VMEM)] + specs,
            out_specs=(out_spec,) * 4 + (delta_spec,),
            scratch_shapes=scratch,
        ),
        name="forward_second",
    )(info, partner, cache, batch_t, loss, head, head, w, w)


def backward_kernel(
    info,
    leaving,
    cache_ref,
    ids_ref,
    batch_ref,
    delta_a,
    delta_hbm,
    w_a,
    w_b,
    sent_ref,
    acc_ref,
    upd_ref,
    delta_b,
    arrived,
):
    rows, width = cache_ref.shape
    embed = width // 3
    owners, capacity = leaving.shape
    step = pl.program_id(0)
    half = w_a.shape[1]
    copy = pltpu.make_async_copy(delta_hbm, delta_b, arrived)

    @pl.when(step == 0)
    def _():
        copy.start()

    back = lax.dot_general(w_a[...], delta_a[...].reshape(half, -1), NN, preferred_element_type=jnp.float32)

    @pl.when(step == 0)
    def _():
        copy.wait()

    back += lax.dot_general(w_b[...], delta_b[...].reshape(half, -1), NN, preferred_element_type=jnp.float32)
    total = None
    for k in range(w_a.shape[0] // embed):
        part = back[k * embed : (k + 1) * embed]
        high = part.astype(jnp.bfloat16)
        low = (part - high.astype(jnp.float32)).astype(jnp.bfloat16)
        pick = onehot(batch_ref[pl.ds(step * (w_a.shape[0] // embed) + k, 1), :], rows)
        add = lax.dot_general(jnp.concatenate([high, low], 0), pick, NT, preferred_element_type=jnp.float32)
        total = add if total is None else total + add

    @pl.when(step == 0)
    def _():
        acc_ref[...] = total
        sent_ref[:, 3 * capacity :, :] = ids_ref[...]

    @pl.when(step > 0)
    def _():
        acc_ref[...] += total

    @pl.when(step == pl.num_programs(0) - 1)
    def _():
        grads = jnp.transpose(acc_ref[:embed, :] + acc_ref[embed:, :])
        value = cache_ref[:, :embed]
        first = cache_ref[:, embed : 2 * embed]
        second = cache_ref[:, 2 * embed :]
        first = beta_one * first + (1.0 - beta_one) * grads
        second = beta_two * second + (1.0 - beta_two) * grads * grads
        upd_ref[:, :embed] = value - learn_rate * (first / bias_one) / (jnp.sqrt(second / bias_two) + epsilon)
        upd_ref[:, embed : 2 * embed] = first
        upd_ref[:, 2 * embed :] = second

        def evict(i, carry):
            for k in range(capacity):
                row = upd_ref[pl.ds(leaving[i, k], 1), :]
                for p in range(3):
                    at = p * capacity + k
                    sent_ref[i, at : at + 1, :] = row[:, p * embed : (p + 1) * embed]
            return carry

        lax.fori_loop(0, owners, evict, 0)


def backward(info, leaving, cache, ids, batch_t, delta_a, delta_b, w):
    rows, width3 = cache.shape
    embed = width3 // 3
    features, _ = batch_t.shape
    width = w.shape[0]
    half = width // 2
    steps = features // 2
    owners, capacity = leaving.shape
    fixed = lambda shape: pl.BlockSpec(shape, lambda j, c, e: tuple(0 for _ in shape))
    whole = pl.BlockSpec(memory_space=pltpu.VMEM)
    sent = (owners, 3 * capacity + ids.shape[1], embed)
    return pl.pallas_call(
        backward_kernel,
        out_shape=jax.ShapeDtypeStruct(sent, jnp.float32),
        grid_spec=pltpu.PrefetchScalarGridSpec(
            num_scalar_prefetch=2,
            grid=(steps,),
            in_specs=[
                fixed(cache.shape),
                fixed(ids.shape),
                fixed(batch_t.shape),
                whole,
                pl.BlockSpec(memory_space=pl.ANY),
                pl.BlockSpec((2 * embed, half), lambda j, c, e: (j, c[0])),
                pl.BlockSpec((2 * embed, half), lambda j, c, e: (j, c[1])),
            ],
            out_specs=fixed(sent),
            scratch_shapes=[
                pltpu.VMEM((2 * embed, rows), jnp.float32),
                pltpu.VMEM((rows, width3), jnp.float32),
                pltpu.VMEM(delta_b.shape, delta_b.dtype),
                pltpu.SemaphoreType.DMA(()),
            ],
        ),
        name="backward",
    )(info, leaving, cache, ids, batch_t, delta_a, delta_b, w, w)


def serve_kernel(asked_ref, table_ref, out_ref):
    owners, both = asked_ref.shape
    capacity = both // 2
    embed = out_ref.shape[2]
    out_ref[:, 3 * capacity :, :] = jnp.zeros((owners, out_ref.shape[1] - 3 * capacity, embed), out_ref.dtype)

    def fetch(i, carry):
        for k in range(capacity):
            row = table_ref[pl.ds(asked_ref[i, k], 1), :]
            for p in range(3):
                at = p * capacity + k
                out_ref[i, at : at + 1, :] = row[:, p * embed : (p + 1) * embed]
        return carry

    lax.fori_loop(0, owners, fetch, 0)


def serve(asked, table, rows):
    owners, both = asked.shape
    return pl.pallas_call(
        serve_kernel,
        out_shape=jax.ShapeDtypeStruct((owners, 3 * both // 2 + rows, table.shape[1] // 3), jnp.float32),
        in_specs=[pl.BlockSpec(memory_space=pltpu.SMEM), pl.BlockSpec(table.shape)],
        name="serve",
    )(asked, table)


def block_kernel(mine_ref, other_ref, served_ref, out_ref):
    rows = mine_ref.shape[2]
    for k in range(2):
        out_ref[:, k * rows : (k + 1) * rows, :] = mine_ref[k] + other_ref[k]


def add_block(mine, other, served):
    colours, owners, rows, embed = other.shape
    whole = pl.BlockSpec(memory_space=pltpu.VMEM)
    block = colours * rows
    return pl.pallas_call(
        block_kernel,
        out_shape=jax.ShapeDtypeStruct(served.shape, served.dtype),
        grid=(1,),
        in_specs=[whole, whole, pl.BlockSpec(memory_space=pl.ANY)],
        out_specs=pl.BlockSpec((owners, block, embed), lambda j: (0, served.shape[1] // block - 1, 0)),
        input_output_aliases={2: 0},
        name="add_block",
    )(mine, other, served)


def lookup_kernel(home_ref, wanted_ref, gone_ref, counts_ref, out_ref, *, table_rows):
    owners, capacity = wanted_ref.shape

    def look(i, carry):
        count = counts_ref[0, i]
        for k in range(capacity):
            out_ref[i, k] = home_ref[0, wanted_ref[i, k]] & (table_rows - 1)
            slot = home_ref[0, gone_ref[i, k]] & (table_rows - 1)
            out_ref[i, capacity + k] = jnp.where(k < count, slot, table_rows)
        return carry

    lax.fori_loop(0, owners, look, 0)


def lookup(home, wanted, gone, counts, table_rows):
    owners, capacity = wanted.shape
    scalar = pl.BlockSpec(memory_space=pltpu.SMEM)
    return pl.pallas_call(
        functools.partial(lookup_kernel, table_rows=table_rows),
        out_shape=jax.ShapeDtypeStruct((owners, 2 * capacity), jnp.int32),
        in_specs=[scalar] * 4,
        out_specs=scalar,
        name="lookup",
    )(home, wanted, gone, counts)


def share_kernel(got_ref, out_ref):
    rows = out_ref.shape[1]
    last = pl.ds(got_ref.shape[1] - rows, rows)
    total = got_ref[0, last]
    for i in range(1, got_ref.shape[0]):
        total += got_ref[i, last]
    for d in range(out_ref.shape[0]):
        out_ref[d] = total


def share_total(got, rows, devices):
    return pl.pallas_call(
        share_kernel,
        out_shape=jax.ShapeDtypeStruct((devices, rows, got.shape[2]), got.dtype),
        in_specs=[pl.BlockSpec(memory_space=pltpu.VMEM)],
        name="share_total",
    )(got)


def settle_kernel(asked_ref, got_ref, table_ref, new_ref, rows_ref):
    owners, both = asked_ref.shape
    capacity = both // 2
    embed = got_ref.shape[2]
    table_rows = table_ref.shape[0]
    for p in range(3):
        rows_ref[p, :table_rows] = table_ref[:, p * embed : (p + 1) * embed]

    def place(i, carry):
        for k in range(capacity):
            slot = asked_ref[i, capacity + k]
            for p in range(3):
                at = p * capacity + k
                rows_ref[p, pl.ds(slot, 1), :] = got_ref[i, at : at + 1, :]
        return carry

    lax.fori_loop(0, owners, place, 0)
    for p in range(3):
        new_ref[:, p * embed : (p + 1) * embed] = rows_ref[p, :table_rows]


def settle(asked, got, table):
    table_rows, width = table.shape
    return pl.pallas_call(
        settle_kernel,
        out_shape=jax.ShapeDtypeStruct(table.shape, table.dtype),
        in_specs=[
            pl.BlockSpec(memory_space=pltpu.SMEM),
            pl.BlockSpec(memory_space=pltpu.VMEM),
            pl.BlockSpec(table.shape),
        ],
        out_specs=pl.BlockSpec(table.shape),
        scratch_shapes=[pltpu.VMEM((3, table_rows + 8, width // 3), table.dtype)],
        name="settle",
    )(asked, got, table)


def mask_kernel(counts_ref, got_ref, fetched_ref):
    owners, capacity, width = fetched_ref.shape
    embed = width // 3
    for i in range(owners):
        live = lax.broadcasted_iota(jnp.int32, (capacity, embed), 0) < counts_ref[0, i]
        for p in range(3):
            block = got_ref[i, p * capacity : (p + 1) * capacity, :]
            fetched_ref[i, :, p * embed : (p + 1) * embed] = jnp.where(live, block, 0.0)


def mask_rows(counts, got, capacity):
    return pl.pallas_call(
        mask_kernel,
        out_shape=jax.ShapeDtypeStruct((got.shape[0], capacity, 3 * got.shape[2]), got.dtype),
        in_specs=[pl.BlockSpec(memory_space=pltpu.SMEM), pl.BlockSpec(memory_space=pltpu.VMEM)],
        name="mask_rows",
    )(counts, got)


def finish_kernel(every_ref, out_ref, *, scale):
    _, both, columns = every_ref.shape
    rows = both // 2
    for x in range(side):
        for c in range(2):
            left = (c * side + x) * columns
            for k in range(2):
                for y in range(0, side, 2):
                    pair = [every_ref[(x * side + y + i) * 2 + c, k * rows : (k + 1) * rows] for i in range(2)]
                    top = (k * side + y) * rows
                    out_ref[top : top + both, left : left + columns] = (
                        jnp.concatenate(pair, 0) * scale
                    ).astype(out_ref.dtype)


def finish(every, scale):
    _, rows, columns = every.shape
    return pl.pallas_call(
        functools.partial(finish_kernel, scale=scale),
        out_shape=jax.ShapeDtypeStruct((side * rows, 2 * side * columns), jnp.bfloat16),
        in_specs=[pl.BlockSpec(memory_space=pltpu.VMEM)],
        name="finish",
    )(every)


def pairs(core, x, y):
    bits = (x * side + y) * 2 + core
    return [(d, d ^ bits) for d in range(2 * side * side)]


def send_to(a, x, y):
    return lax.ppermute(a, "dp", pairs(0, x, y))


def on_chip(a):
    return pltpu.with_memory_space_constraint(a, pltpu.VMEM)


def local(
    cache_state,
    table_state,
    batch_idx,
    loss_grad,
    w_first,
    head,
    home,
    fetch_rows,
    fetch_counts,
    evict_rows,
    evict_from,
    evict_counts,
):
    group = lax.axis_size("shard")
    devices = lax.axis_size("dp")
    place = lax.axis_index("dp").astype(jnp.uint32)
    core = (place & 1).astype(jnp.int32)
    cache = cache_state[0, 0]
    table = table_state[0, 0]
    batch_t = batch_idx[0, 0].T
    loss = loss_grad[0]
    wanted = fetch_rows[0, 0]
    gone = evict_rows[0, 0]
    table_rows = table.shape[0]
    capacity = wanted.shape[1]
    samples = loss.shape[1]
    mlp_width = w_first.shape[0]

    info = jnp.stack([1 - core, core, (place >> 3).astype(jnp.int32), ((place >> 1) & 3).astype(jnp.int32)])
    head_row = head[None]
    send, delta_a = forward_half(info, group, cache, batch_t, None, loss, head_row, w_first)
    partner = on_chip(lax.ppermute(send, "dp", pairs(1, 0, 0)))
    slots = lookup(home, wanted, gone, evict_counts[0], table_rows)
    lanes = cache.shape[1] // 3
    ids = jnp.pad(slots.astype(jnp.float32), ((0, 0), (0, lanes - slots.shape[1])))
    ids = jnp.broadcast_to(ids[:, None, :], (group, 8, lanes))
    loss, ids = lax.optimization_barrier((loss, ids))
    even, even_out, odd, odd_out, delta_b = forward_half(info, group, cache, batch_t, partner, loss, head_row, w_first)
    even_in = send_to(even_out, 1, 0)
    odd_in = send_to(odd_out, 0, 1)
    sent = backward(info, evict_from[0, 0], cache, ids, batch_t, on_chip(delta_a), delta_b, w_first)
    got = lax.all_to_all(sent, "shard", split_axis=0, concat_axis=0, tiled=True)
    even = even[0] + even_in[0] + send_to(even[1] + even_in[1], 0, 1)
    odd = odd[0] + odd_in[0] + send_to(odd[1] + odd_in[1], 1, 0)
    mine = jnp.stack([even[0], odd[0]], 1) + send_to(jnp.stack([even[1], odd[1]], 1), 3, 0)
    other = send_to(mine[1], 0, 3)
    asked = got[:, 3 * capacity, : 2 * capacity].astype(jnp.int32)
    served = serve(asked, table, 2 * mine.shape[3])
    served = add_block(on_chip(mine[0]), on_chip(other), served)
    came = on_chip(lax.all_to_all(served, "shard", split_axis=0, concat_axis=0, tiled=True))
    new_table = settle(asked, on_chip(got), table)
    scale = 1.0 / math.sqrt(samples * group * devices)
    every = share_total(came, mlp_width // (group * side), devices)
    every = on_chip(lax.all_to_all(every, "dp", split_axis=0, concat_axis=0, tiled=True))
    fetched = mask_rows(fetch_counts[0], came, capacity)
    grad_first = finish(every, scale)
    return (grad_first, new_table[None, None], fetched[None, None])


def solution(mesh):
    placed = (
        P("dp", "shard", None, None),
        P("dp", "shard", None, None),
        P("dp", "shard", None, None),
        P("dp", "shard", None),
        P(),
        P(),
        P("dp", None),
        P("dp", "shard", None, None),
        P("dp", "shard", None),
        P("dp", "shard", None, None),
        P("dp", "shard", None, None),
        P("dp", "shard", None),
    )

    return jax.shard_map(
        local,
        mesh=mesh,
        in_specs=placed,
        out_specs=(
            P("shard", None),
            P("dp", "shard", None, None),
            P("dp", "shard", None, None, None),
        ),
        check_vma=False,
    )
```

```python
import functools
import math

import jax
import jax.numpy as jnp
from jax import lax
from jax.experimental import pallas as pl
from jax.experimental.pallas import tpu as pltpu
from jax.sharding import PartitionSpec as P


beta_one = 0.9
beta_two = 0.999
learn_rate = 0.05
epsilon = 1e-08
bias_one = 1.0 - 0.9**10
bias_two = 1.0 - 0.999**10
NN = (((1,), (0,)), ((), ()))
NT = (((1,), (1,)), ((), ()))
TN = (((0,), (0,)), ((), ()))
side = 4


def full(shape):
    return pl.BlockSpec(shape, lambda j, o: tuple(0 for _ in shape))


def column(row):
    return jnp.transpose(jnp.broadcast_to(row, (8, row.shape[1])))[:, :1]


def onehot(batch_row, rows):
    shape = (rows, batch_row.shape[1])
    row = lax.broadcasted_iota(jnp.int32, shape, 0).astype(jnp.float32).astype(jnp.bfloat16)
    hit = row == batch_row.astype(jnp.float32).astype(jnp.bfloat16)
    return jnp.where(hit, jnp.ones((), jnp.bfloat16), jnp.zeros((), jnp.bfloat16))


def turn(outer, inner):
    return (3 * outer) ^ inner


def hidden(j, info, inputs, loss, head, w, delta_ref):
    pre = lax.dot_general(w, inputs, TN, preferred_element_type=jnp.float32)
    sigma = jax.nn.sigmoid(pre)
    delta = (loss * column(head) * sigma * (1.0 + pre * (1.0 - sigma))).astype(jnp.bfloat16)
    for u in range(2):
        delta_ref[(turn(j, u) ^ info[2]) & 1] = delta[u * (delta.shape[0] // 2) : (u + 1) * (delta.shape[0] // 2)]
    return lax.dot_general(inputs, delta, NT, preferred_element_type=jnp.float32)


def store_pieces(info, grad_ref, out_ref):
    owners, rows, columns = out_ref.shape[-3:]
    deep = 2 * side * rows
    for v in range(2):
        for o in range(2):
            y = turn(o, v) ^ info[3]
            for u in range(2):
                left = slice(u * columns, (u + 1) * columns)
                for z in range(owners):
                    even = pl.multiple_of(z * deep + y * rows, rows)
                    odd = pl.multiple_of(z * deep + side * rows + y * rows, rows)
                    out_ref[u, v, 0, o, z] = grad_ref[pl.ds(even, rows), left]
                    out_ref[2 + v, u, 0, o, z] = grad_ref[pl.ds(odd, rows), left]


def forward_kernel(
    info,
    cache_ref,
    batch_ref,
    loss_ref,
    head_a,
    head_b,
    w_a,
    w_b,
    send_ref,
    keep_ref,
    delta_a,
    delta_b,
    inputs_ref,
    grad_ref,
):
    rows = cache_ref.shape[0]
    features = batch_ref.shape[0]
    embed = inputs_ref.shape[0] // features
    step = pl.program_id(0)
    j = step & 1

    @pl.when(step == 0)
    def _():
        looked = jnp.transpose(cache_ref[...]).astype(jnp.bfloat16)
        for f in range(features):
            pick = onehot(batch_ref[f : f + 1, :], rows)
            inputs_ref[f * embed : (f + 1) * embed, :] = lax.dot_general(
                looked, pick, NN, preferred_element_type=jnp.float32
            ).astype(jnp.bfloat16)

    head = jnp.concatenate([head_a[...], head_b[...]], 1)
    w = jnp.concatenate([w_a[...], w_b[...]], 1)

    @pl.when(step < 2)
    def _():
        grad_ref[...] = hidden(j, info, inputs_ref[...], loss_ref[...], head, w, delta_a)
        store_pieces(info, grad_ref, send_ref)

    @pl.when(step >= 2)
    def _():
        grad_ref[...] = hidden(j, info, inputs_ref[...], loss_ref[...], head, w, delta_b)
        store_pieces(info, grad_ref, keep_ref)


def forward(info, owners, cache, batch_t, loss, head, w):
    samples = loss.shape[1]
    width = w.shape[0]
    half = width // 2
    block = half // side
    rows = cache.shape[0]
    embed = cache.shape[1] // 3
    part = lambda u: lambda i, c: (0, side * c[i >> 1] + (turn(i & 1, u) ^ c[2]))
    specs = [pl.BlockSpec((rows, embed), lambda i, c: (0, 0)), full(batch_t.shape), full((1, samples))]
    specs += [pl.BlockSpec((1, block), part(u)) for u in range(2)]
    specs += [pl.BlockSpec((width, block), part(u)) for u in range(2)]
    piece = (4, 2, 2, 2, owners, width // (owners * 2 * side), block)
    grad = jax.ShapeDtypeStruct(piece, jnp.float32)
    delta = jax.ShapeDtypeStruct((side, block, samples), jnp.bfloat16)
    early = lambda i: jnp.minimum(i, 1)
    late = lambda i: jnp.maximum(i - 2, 0)
    grad_spec = lambda at: pl.BlockSpec((4, 2, 1) + piece[3:], lambda i, c: (0, 0, at(i), 0, 0, 0, 0))
    delta_spec = lambda at: pl.BlockSpec((2, block, samples), lambda i, c: (at(i) ^ (c[2] >> 1), 0, 0))
    return pl.pallas_call(
        forward_kernel,
        out_shape=(grad, grad, delta, delta),
        grid_spec=pltpu.PrefetchScalarGridSpec(
            num_scalar_prefetch=1,
            grid=(4,),
            in_specs=specs,
            out_specs=(grad_spec(early), grad_spec(late), delta_spec(early), delta_spec(late)),
            scratch_shapes=[pltpu.VMEM((width, samples), jnp.bfloat16), pltpu.VMEM((width, 2 * block), jnp.float32)],
        ),
        name="forward",
    )(info, cache, batch_t, loss, head, head, w, w)


def backward_kernel(
    info,
    leaving,
    cache_ref,
    ids_ref,
    batch_ref,
    delta_a,
    delta_hbm,
    w_a,
    w_b,
    sent_ref,
    acc_ref,
    upd_ref,
    delta_b,
    arrived,
):
    rows, width = cache_ref.shape
    embed = width // 3
    owners, capacity = leaving.shape
    step = pl.program_id(0)
    half = w_a.shape[1]
    copy = pltpu.make_async_copy(delta_hbm, delta_b, arrived)

    @pl.when(step == 0)
    def _():
        copy.start()

    back = lax.dot_general(w_a[...], delta_a[...].reshape(half, -1), NN, preferred_element_type=jnp.float32)

    @pl.when(step == 0)
    def _():
        copy.wait()

    back += lax.dot_general(w_b[...], delta_b[...].reshape(half, -1), NN, preferred_element_type=jnp.float32)
    total = None
    for k in range(w_a.shape[0] // embed):
        part = back[k * embed : (k + 1) * embed]
        high = part.astype(jnp.bfloat16)
        low = (part - high.astype(jnp.float32)).astype(jnp.bfloat16)
        pick = onehot(batch_ref[pl.ds(step * (w_a.shape[0] // embed) + k, 1), :], rows)
        add = lax.dot_general(jnp.concatenate([high, low], 0), pick, NT, preferred_element_type=jnp.float32)
        total = add if total is None else total + add

    @pl.when(step == 0)
    def _():
        acc_ref[...] = total
        sent_ref[:, 3 * capacity :, :] = ids_ref[...]

    @pl.when(step > 0)
    def _():
        acc_ref[...] += total

    @pl.when(step == pl.num_programs(0) - 1)
    def _():
        grads = jnp.transpose(acc_ref[:embed, :] + acc_ref[embed:, :])
        value = cache_ref[:, :embed]
        first = cache_ref[:, embed : 2 * embed]
        second = cache_ref[:, 2 * embed :]
        first = beta_one * first + (1.0 - beta_one) * grads
        second = beta_two * second + (1.0 - beta_two) * grads * grads
        upd_ref[:, :embed] = value - learn_rate * (first / bias_one) / (jnp.sqrt(second / bias_two) + epsilon)
        upd_ref[:, embed : 2 * embed] = first
        upd_ref[:, 2 * embed :] = second

        def evict(i, carry):
            for k in range(capacity):
                row = upd_ref[pl.ds(leaving[i, k], 1), :]
                for p in range(3):
                    at = p * capacity + k
                    sent_ref[i, at : at + 1, :] = row[:, p * embed : (p + 1) * embed]
            return carry

        lax.fori_loop(0, owners, evict, 0)


def backward(info, leaving, cache, ids, batch_t, delta_a, delta_b, w):
    rows, width3 = cache.shape
    embed = width3 // 3
    features, _ = batch_t.shape
    width = w.shape[0]
    half = width // 2
    steps = features // 2
    owners, capacity = leaving.shape
    fixed = lambda shape: pl.BlockSpec(shape, lambda j, c, e: tuple(0 for _ in shape))
    whole = pl.BlockSpec(memory_space=pltpu.VMEM)
    sent = (owners, 3 * capacity + ids.shape[1], embed)
    return pl.pallas_call(
        backward_kernel,
        out_shape=jax.ShapeDtypeStruct(sent, jnp.float32),
        grid_spec=pltpu.PrefetchScalarGridSpec(
            num_scalar_prefetch=2,
            grid=(steps,),
            in_specs=[
                fixed(cache.shape),
                fixed(ids.shape),
                fixed(batch_t.shape),
                whole,
                pl.BlockSpec(memory_space=pl.ANY),
                pl.BlockSpec((2 * embed, half), lambda j, c, e: (j, c[0])),
                pl.BlockSpec((2 * embed, half), lambda j, c, e: (j, c[1])),
            ],
            out_specs=fixed(sent),
            scratch_shapes=[
                pltpu.VMEM((2 * embed, rows), jnp.float32),
                pltpu.VMEM((rows, width3), jnp.float32),
                pltpu.VMEM(delta_b.shape, delta_b.dtype),
                pltpu.SemaphoreType.DMA(()),
            ],
        ),
        name="backward",
    )(info, leaving, cache, ids, batch_t, delta_a, delta_b, w, w)


def serve_kernel(asked_ref, table_ref, out_ref):
    owners, both = asked_ref.shape
    capacity = both // 2
    embed = out_ref.shape[2]
    out_ref[:, 3 * capacity :, :] = jnp.zeros((owners, out_ref.shape[1] - 3 * capacity, embed), out_ref.dtype)

    def fetch(i, carry):
        for k in range(capacity):
            row = table_ref[pl.ds(asked_ref[i, k], 1), :]
            for p in range(3):
                at = p * capacity + k
                out_ref[i, at : at + 1, :] = row[:, p * embed : (p + 1) * embed]
        return carry

    lax.fori_loop(0, owners, fetch, 0)


def serve(asked, table, rows):
    owners, both = asked.shape
    return pl.pallas_call(
        serve_kernel,
        out_shape=jax.ShapeDtypeStruct((owners, 3 * both // 2 + rows, table.shape[1] // 3), jnp.float32),
        in_specs=[pl.BlockSpec(memory_space=pltpu.SMEM), pl.BlockSpec(table.shape)],
        name="serve",
    )(asked, table)


def block_kernel(mine_ref, other_ref, served_ref, out_ref):
    rows = mine_ref.shape[2]
    for k in range(2):
        out_ref[:, k * rows : (k + 1) * rows, :] = mine_ref[k] + other_ref[k]


def add_block(mine, other, served):
    colours, owners, rows, embed = other.shape
    whole = pl.BlockSpec(memory_space=pltpu.VMEM)
    block = colours * rows
    return pl.pallas_call(
        block_kernel,
        out_shape=jax.ShapeDtypeStruct(served.shape, served.dtype),
        grid=(1,),
        in_specs=[whole, whole, pl.BlockSpec(memory_space=pl.ANY)],
        out_specs=pl.BlockSpec((owners, block, embed), lambda j: (0, served.shape[1] // block - 1, 0)),
        input_output_aliases={2: 0},
        name="add_block",
    )(mine, other, served)


def lookup_kernel(home_ref, wanted_ref, gone_ref, counts_ref, out_ref, *, table_rows):
    owners, capacity = wanted_ref.shape

    def look(i, carry):
        count = counts_ref[0, i]
        for k in range(capacity):
            out_ref[i, k] = home_ref[0, wanted_ref[i, k]] & (table_rows - 1)
            slot = home_ref[0, gone_ref[i, k]] & (table_rows - 1)
            out_ref[i, capacity + k] = jnp.where(k < count, slot, table_rows)
        return carry

    lax.fori_loop(0, owners, look, 0)


def lookup(home, wanted, gone, counts, table_rows):
    owners, capacity = wanted.shape
    scalar = pl.BlockSpec(memory_space=pltpu.SMEM)
    return pl.pallas_call(
        functools.partial(lookup_kernel, table_rows=table_rows),
        out_shape=jax.ShapeDtypeStruct((owners, 2 * capacity), jnp.int32),
        in_specs=[scalar] * 4,
        out_specs=scalar,
        name="lookup",
    )(home, wanted, gone, counts)


def share_kernel(got_ref, out_ref):
    rows = out_ref.shape[1]
    last = pl.ds(got_ref.shape[1] - rows, rows)
    total = got_ref[0, last]
    for i in range(1, got_ref.shape[0]):
        total += got_ref[i, last]
    for d in range(out_ref.shape[0]):
        out_ref[d] = total


def share_total(got, rows, devices):
    return pl.pallas_call(
        share_kernel,
        out_shape=jax.ShapeDtypeStruct((devices, rows, got.shape[2]), got.dtype),
        in_specs=[pl.BlockSpec(memory_space=pltpu.VMEM)],
        name="share_total",
    )(got)


def settle_kernel(asked_ref, got_ref, table_ref, new_ref, rows_ref):
    owners, both = asked_ref.shape
    capacity = both // 2
    embed = got_ref.shape[2]
    table_rows = table_ref.shape[0]
    for p in range(3):
        rows_ref[p, :table_rows] = table_ref[:, p * embed : (p + 1) * embed]

    def place(i, carry):
        for k in range(capacity):
            slot = asked_ref[i, capacity + k]
            for p in range(3):
                at = p * capacity + k
                rows_ref[p, pl.ds(slot, 1), :] = got_ref[i, at : at + 1, :]
        return carry

    lax.fori_loop(0, owners, place, 0)
    for p in range(3):
        new_ref[:, p * embed : (p + 1) * embed] = rows_ref[p, :table_rows]


def settle(asked, got, table):
    table_rows, width = table.shape
    return pl.pallas_call(
        settle_kernel,
        out_shape=jax.ShapeDtypeStruct(table.shape, table.dtype),
        in_specs=[
            pl.BlockSpec(memory_space=pltpu.SMEM),
            pl.BlockSpec(memory_space=pltpu.VMEM),
            pl.BlockSpec(table.shape),
        ],
        out_specs=pl.BlockSpec(table.shape),
        scratch_shapes=[pltpu.VMEM((3, table_rows + 8, width // 3), table.dtype)],
        name="settle",
    )(asked, got, table)


def mask_kernel(counts_ref, got_ref, fetched_ref):
    owners, capacity, width = fetched_ref.shape
    embed = width // 3
    for i in range(owners):
        live = lax.broadcasted_iota(jnp.int32, (capacity, embed), 0) < counts_ref[0, i]
        for p in range(3):
            block = got_ref[i, p * capacity : (p + 1) * capacity, :]
            fetched_ref[i, :, p * embed : (p + 1) * embed] = jnp.where(live, block, 0.0)


def mask_rows(counts, got, capacity):
    return pl.pallas_call(
        mask_kernel,
        out_shape=jax.ShapeDtypeStruct((got.shape[0], capacity, 3 * got.shape[2]), got.dtype),
        in_specs=[pl.BlockSpec(memory_space=pltpu.SMEM), pl.BlockSpec(memory_space=pltpu.VMEM)],
        name="mask_rows",
    )(counts, got)


def finish_kernel(every_ref, out_ref, *, scale):
    _, both, columns = every_ref.shape
    rows = both // 2
    for x in range(side):
        for c in range(2):
            left = (c * side + x) * columns
            for k in range(2):
                for y in range(0, side, 2):
                    pair = [every_ref[(x * side + y + i) * 2 + c, k * rows : (k + 1) * rows] for i in range(2)]
                    top = (k * side + y) * rows
                    out_ref[top : top + both, left : left + columns] = (
                        jnp.concatenate(pair, 0) * scale
                    ).astype(out_ref.dtype)


def finish(every, scale):
    _, rows, columns = every.shape
    return pl.pallas_call(
        functools.partial(finish_kernel, scale=scale),
        out_shape=jax.ShapeDtypeStruct((side * rows, 2 * side * columns), jnp.bfloat16),
        in_specs=[pl.BlockSpec(memory_space=pltpu.VMEM)],
        name="finish",
    )(every)


def pairs(core, x, y):
    bits = (x * side + y) * 2 + core
    return [(d, d ^ bits) for d in range(2 * side * side)]


def send_to(a, x, y):
    return lax.ppermute(a, "dp", pairs(0, x, y))


def on_chip(a):
    return pltpu.with_memory_space_constraint(a, pltpu.VMEM)


def local(
    cache_state,
    table_state,
    batch_idx,
    loss_grad,
    w_first,
    head,
    home,
    fetch_rows,
    fetch_counts,
    evict_rows,
    evict_from,
    evict_counts,
):
    group = lax.axis_size("shard")
    devices = lax.axis_size("dp")
    place = lax.axis_index("dp").astype(jnp.uint32)
    core = (place & 1).astype(jnp.int32)
    cache = cache_state[0, 0]
    table = table_state[0, 0]
    batch_t = batch_idx[0, 0].T
    loss = loss_grad[0]
    wanted = fetch_rows[0, 0]
    gone = evict_rows[0, 0]
    table_rows = table.shape[0]
    capacity = wanted.shape[1]
    samples = loss.shape[1]
    mlp_width = w_first.shape[0]

    info = jnp.stack([1 - core, core, (place >> 3).astype(jnp.int32), ((place >> 1) & 3).astype(jnp.int32)])
    head_row = head[None]
    send, keep, delta_a, delta_b = forward(info, group, cache, batch_t, loss, head_row, w_first)
    partner = lax.ppermute(send, "dp", pairs(1, 0, 0))
    slots = lookup(home, wanted, gone, evict_counts[0], table_rows)
    lanes = cache.shape[1] // 3
    ids = jnp.pad(slots.astype(jnp.float32), ((0, 0), (0, lanes - slots.shape[1])))
    ids = jnp.broadcast_to(ids[:, None, :], (group, 8, lanes))
    partner, ids = lax.optimization_barrier((partner, ids))
    even_in = send_to(keep[1] + partner[1], 1, 0)
    odd_in = send_to(keep[3] + partner[3], 0, 1)
    sent = backward(info, evict_from[0, 0], cache, ids, batch_t, on_chip(delta_a), delta_b, w_first)
    got = lax.all_to_all(sent, "shard", split_axis=0, concat_axis=0, tiled=True)
    even = keep[0] + partner[0] + even_in
    odd = keep[2] + partner[2] + odd_in
    even = even[0] + send_to(even[1], 0, 1)
    odd = odd[0] + send_to(odd[1], 1, 0)
    mine = jnp.stack([even[0], odd[0]], 1) + send_to(jnp.stack([even[1], odd[1]], 1), 3, 0)
    other = send_to(mine[1], 0, 3)
    asked = got[:, 3 * capacity, : 2 * capacity].astype(jnp.int32)
    served = serve(asked, table, 2 * mine.shape[3])
    served = add_block(on_chip(mine[0]), on_chip(other), served)
    came = on_chip(lax.all_to_all(served, "shard", split_axis=0, concat_axis=0, tiled=True))
    new_table = settle(asked, on_chip(got), table)
    scale = 1.0 / math.sqrt(samples * group * devices)
    every = share_total(came, mlp_width // (group * side), devices)
    every = on_chip(lax.all_to_all(every, "dp", split_axis=0, concat_axis=0, tiled=True))
    fetched = mask_rows(fetch_counts[0], came, capacity)
    grad_first = finish(every, scale)
    return (grad_first, new_table[None, None], fetched[None, None])


def solution(mesh):
    placed = (
        P("dp", "shard", None, None),
        P("dp", "shard", None, None),
        P("dp", "shard", None, None),
        P("dp", "shard", None),
        P(),
        P(),
        P("dp", None),
        P("dp", "shard", None, None),
        P("dp", "shard", None),
        P("dp", "shard", None, None),
        P("dp", "shard", None, None),
        P("dp", "shard", None),
    )

    return jax.shard_map(
        local,
        mesh=mesh,
        in_specs=placed,
        out_specs=(
            P("shard", None),
            P("dp", "shard", None, None),
            P("dp", "shard", None, None, None),
        ),
        check_vma=False,
    )
```

```python
import functools
import math

import jax
import jax.numpy as jnp
from jax import lax
from jax.experimental import pallas as pl
from jax.experimental.pallas import tpu as pltpu
from jax.sharding import PartitionSpec as P


beta_one = 0.9
beta_two = 0.999
learn_rate = 0.05
epsilon = 1e-08
bias_one = 1.0 - 0.9**10
bias_two = 1.0 - 0.999**10
NN = (((1,), (0,)), ((), ()))
NT = (((1,), (1,)), ((), ()))
TN = (((0,), (0,)), ((), ()))
side = 4


def full(shape):
    return pl.BlockSpec(shape, lambda j, o: tuple(0 for _ in shape))


def column(row):
    return jnp.transpose(jnp.broadcast_to(row, (8, row.shape[1])))[:, :1]


def onehot(batch_row, rows):
    shape = (rows, batch_row.shape[1])
    row = lax.broadcasted_iota(jnp.int32, shape, 0).astype(jnp.float32).astype(jnp.bfloat16)
    hit = row == batch_row.astype(jnp.float32).astype(jnp.bfloat16)
    return jnp.where(hit, jnp.ones((), jnp.bfloat16), jnp.zeros((), jnp.bfloat16))


def turn(outer, inner):
    return (3 * outer) ^ inner


def hidden(j, info, inputs, loss, head, w, delta_ref):
    pre = lax.dot_general(w, inputs, TN, preferred_element_type=jnp.float32)
    sigma = jax.nn.sigmoid(pre)
    delta = (loss * column(head) * sigma * (1.0 + pre * (1.0 - sigma))).astype(jnp.bfloat16)
    for u in range(2):
        delta_ref[(turn(j, u) ^ info[2]) & 1] = delta[u * (delta.shape[0] // 2) : (u + 1) * (delta.shape[0] // 2)]
    return lax.dot_general(inputs, delta, NT, preferred_element_type=jnp.float32)


def store_pieces(info, grad_ref, out_ref):
    owners, rows, columns = out_ref.shape[-3:]
    deep = 2 * side * rows
    for v in range(2):
        for o in range(2):
            y = turn(o, v) ^ info[3]
            for u in range(2):
                left = slice(u * columns, (u + 1) * columns)
                for z in range(owners):
                    even = pl.multiple_of(z * deep + y * rows, rows)
                    odd = pl.multiple_of(z * deep + side * rows + y * rows, rows)
                    out_ref[u, v, 0, o, z] = grad_ref[pl.ds(even, rows), left]
                    out_ref[2 + v, u, 0, o, z] = grad_ref[pl.ds(odd, rows), left]


def forward_kernel(
    info,
    cache_ref,
    batch_ref,
    loss_ref,
    head_a,
    head_b,
    w_a,
    w_b,
    send_ref,
    keep_ref,
    delta_a,
    delta_b,
    inputs_ref,
    grad_ref,
):
    rows = cache_ref.shape[0]
    features = batch_ref.shape[0]
    embed = inputs_ref.shape[0] // features
    step = pl.program_id(0)
    j = step & 1

    @pl.when(step == 0)
    def _():
        looked = jnp.transpose(cache_ref[...]).astype(jnp.bfloat16)
        for f in range(features):
            pick = onehot(batch_ref[f : f + 1, :], rows)
            inputs_ref[f * embed : (f + 1) * embed, :] = lax.dot_general(
                looked, pick, NN, preferred_element_type=jnp.float32
            ).astype(jnp.bfloat16)

    head = jnp.concatenate([head_a[...], head_b[...]], 1)
    w = jnp.concatenate([w_a[...], w_b[...]], 1)

    @pl.when(step < 2)
    def _():
        grad_ref[...] = hidden(j, info, inputs_ref[...], loss_ref[...], head, w, delta_a)
        store_pieces(info, grad_ref, send_ref)

    @pl.when(step >= 2)
    def _():
        grad_ref[...] = hidden(j, info, inputs_ref[...], loss_ref[...], head, w, delta_b)
        store_pieces(info, grad_ref, keep_ref)


def forward(info, owners, cache, batch_t, loss, head, w):
    samples = loss.shape[1]
    width = w.shape[0]
    half = width // 2
    block = half // side
    rows = cache.shape[0]
    embed = cache.shape[1] // 3
    part = lambda u: lambda i, c: (0, side * c[i >> 1] + (turn(i & 1, u) ^ c[2]))
    specs = [pl.BlockSpec((rows, embed), lambda i, c: (0, 0)), full(batch_t.shape), full((1, samples))]
    specs += [pl.BlockSpec((1, block), part(u)) for u in range(2)]
    specs += [pl.BlockSpec((width, block), part(u)) for u in range(2)]
    piece = (4, 2, 2, 2, owners, width // (owners * 2 * side), block)
    grad = jax.ShapeDtypeStruct(piece, jnp.float32)
    delta = jax.ShapeDtypeStruct((side, block, samples), jnp.bfloat16)
    early = lambda i: jnp.minimum(i, 1)
    late = lambda i: jnp.maximum(i - 2, 0)
    grad_spec = lambda at: pl.BlockSpec((4, 2, 1) + piece[3:], lambda i, c: (0, 0, at(i), 0, 0, 0, 0))
    delta_spec = lambda at: pl.BlockSpec((2, block, samples), lambda i, c: (at(i) ^ (c[2] >> 1), 0, 0))
    return pl.pallas_call(
        forward_kernel,
        out_shape=(grad, grad, delta, delta),
        grid_spec=pltpu.PrefetchScalarGridSpec(
            num_scalar_prefetch=1,
            grid=(4,),
            in_specs=specs,
            out_specs=(grad_spec(early), grad_spec(late), delta_spec(early), delta_spec(late)),
            scratch_shapes=[pltpu.VMEM((width, samples), jnp.bfloat16), pltpu.VMEM((width, 2 * block), jnp.float32)],
        ),
        name="forward",
    )(info, cache, batch_t, loss, head, head, w, w)


def backward_kernel(
    info,
    leaving,
    cache_ref,
    ids_ref,
    batch_ref,
    delta_a,
    delta_b,
    w_a,
    w_b,
    sent_ref,
    acc_ref,
    upd_ref,
):
    rows, width = cache_ref.shape
    embed = width // 3
    owners, capacity = leaving.shape
    step = pl.program_id(0)
    half = w_a.shape[1]
    back = lax.dot_general(w_a[...], delta_a[...].reshape(half, -1), NN, preferred_element_type=jnp.float32)
    back += lax.dot_general(w_b[...], delta_b[...].reshape(half, -1), NN, preferred_element_type=jnp.float32)
    total = None
    for k in range(w_a.shape[0] // embed):
        part = back[k * embed : (k + 1) * embed]
        high = part.astype(jnp.bfloat16)
        low = (part - high.astype(jnp.float32)).astype(jnp.bfloat16)
        pick = onehot(batch_ref[pl.ds(step * (w_a.shape[0] // embed) + k, 1), :], rows)
        add = lax.dot_general(jnp.concatenate([high, low], 0), pick, NT, preferred_element_type=jnp.float32)
        total = add if total is None else total + add

    @pl.when(step == 0)
    def _():
        acc_ref[...] = total
        spare = sent_ref.shape[1] - 3 * capacity
        sent_ref[:, 3 * capacity :, :] = jnp.zeros((owners, spare, embed), sent_ref.dtype)
        for i in range(owners):
            line = ids_ref[i : i + 1, :].astype(sent_ref.dtype)
            sent_ref[i, 3 * capacity : 3 * capacity + 1, : ids_ref.shape[1]] = line

    @pl.when(step > 0)
    def _():
        acc_ref[...] += total

    @pl.when(step == pl.num_programs(0) - 1)
    def _():
        grads = jnp.transpose(acc_ref[:embed, :] + acc_ref[embed:, :])
        value = cache_ref[:, :embed]
        first = cache_ref[:, embed : 2 * embed]
        second = cache_ref[:, 2 * embed :]
        first = beta_one * first + (1.0 - beta_one) * grads
        second = beta_two * second + (1.0 - beta_two) * grads * grads
        upd_ref[:, :embed] = value - learn_rate * (first / bias_one) / (jnp.sqrt(second / bias_two) + epsilon)
        upd_ref[:, embed : 2 * embed] = first
        upd_ref[:, 2 * embed :] = second

        def evict(i, carry):
            for k in range(capacity):
                row = upd_ref[pl.ds(leaving[i, k], 1), :]
                for p in range(3):
                    at = p * capacity + k
                    sent_ref[i, at : at + 1, :] = row[:, p * embed : (p + 1) * embed]
            return carry

        lax.fori_loop(0, owners, evict, 0)


def backward(info, leaving, cache, ids, batch_t, delta_a, delta_b, w):
    rows, width3 = cache.shape
    embed = width3 // 3
    features, _ = batch_t.shape
    width = w.shape[0]
    half = width // 2
    steps = features // 2
    owners, capacity = leaving.shape
    fixed = lambda shape: pl.BlockSpec(shape, lambda j, c, e: tuple(0 for _ in shape))
    whole = pl.BlockSpec(memory_space=pltpu.VMEM)
    sent = (owners, 3 * capacity + 8, embed)
    return pl.pallas_call(
        backward_kernel,
        out_shape=jax.ShapeDtypeStruct(sent, jnp.float32),
        grid_spec=pltpu.PrefetchScalarGridSpec(
            num_scalar_prefetch=2,
            grid=(steps,),
            in_specs=[
                fixed(cache.shape),
                fixed(ids.shape),
                fixed(batch_t.shape),
                whole,
                whole,
                pl.BlockSpec((2 * embed, half), lambda j, c, e: (j, c[0])),
                pl.BlockSpec((2 * embed, half), lambda j, c, e: (j, c[1])),
            ],
            out_specs=fixed(sent),
            scratch_shapes=[
                pltpu.VMEM((2 * embed, rows), jnp.float32),
                pltpu.VMEM((rows, width3), jnp.float32),
            ],
        ),
        name="backward",
    )(info, leaving, cache, ids, batch_t, delta_a, delta_b, w, w)


def serve_kernel(asked_ref, table_ref, out_ref):
    owners, both = asked_ref.shape
    capacity = both // 2
    embed = out_ref.shape[2]
    out_ref[:, 3 * capacity :, :] = jnp.zeros((owners, out_ref.shape[1] - 3 * capacity, embed), out_ref.dtype)

    def fetch(i, carry):
        for k in range(capacity):
            row = table_ref[pl.ds(asked_ref[i, k], 1), :]
            for p in range(3):
                at = p * capacity + k
                out_ref[i, at : at + 1, :] = row[:, p * embed : (p + 1) * embed]
        return carry

    lax.fori_loop(0, owners, fetch, 0)


def serve(asked, table, rows):
    owners, both = asked.shape
    return pl.pallas_call(
        serve_kernel,
        out_shape=jax.ShapeDtypeStruct((owners, 3 * both // 2 + rows, table.shape[1] // 3), jnp.float32),
        in_specs=[pl.BlockSpec(memory_space=pltpu.SMEM), pl.BlockSpec(table.shape)],
        name="serve",
    )(asked, table)


def block_kernel(mine_ref, other_ref, served_ref, out_ref):
    rows = mine_ref.shape[2]
    for k in range(2):
        out_ref[:, k * rows : (k + 1) * rows, :] = mine_ref[k] + other_ref[k]


def add_block(mine, other, served):
    colours, owners, rows, embed = other.shape
    whole = pl.BlockSpec(memory_space=pltpu.VMEM)
    block = colours * rows
    return pl.pallas_call(
        block_kernel,
        out_shape=jax.ShapeDtypeStruct(served.shape, served.dtype),
        grid=(1,),
        in_specs=[whole, whole, pl.BlockSpec(memory_space=pl.ANY)],
        out_specs=pl.BlockSpec((owners, block, embed), lambda j: (0, served.shape[1] // block - 1, 0)),
        input_output_aliases={2: 0},
        name="add_block",
    )(mine, other, served)


def lookup_kernel(home_ref, wanted_ref, gone_ref, counts_ref, out_ref, *, table_rows):
    owners, capacity = wanted_ref.shape

    def look(i, carry):
        count = counts_ref[0, i]
        for k in range(capacity):
            out_ref[i, k] = home_ref[0, wanted_ref[i, k]] & (table_rows - 1)
            slot = home_ref[0, gone_ref[i, k]] & (table_rows - 1)
            out_ref[i, capacity + k] = jnp.where(k < count, slot, table_rows)
        return carry

    lax.fori_loop(0, owners, look, 0)


def lookup(home, wanted, gone, counts, table_rows):
    owners, capacity = wanted.shape
    scalar = pl.BlockSpec(memory_space=pltpu.SMEM)
    return pl.pallas_call(
        functools.partial(lookup_kernel, table_rows=table_rows),
        out_shape=jax.ShapeDtypeStruct((owners, 2 * capacity), jnp.int32),
        in_specs=[scalar] * 4,
        out_specs=scalar,
        name="lookup",
    )(home, wanted, gone, counts)


def share_kernel(got_ref, out_ref):
    rows = out_ref.shape[1]
    last = pl.ds(got_ref.shape[1] - rows, rows)
    total = got_ref[0, last]
    for i in range(1, got_ref.shape[0]):
        total += got_ref[i, last]
    for d in range(out_ref.shape[0]):
        out_ref[d] = total


def share_total(got, rows, devices):
    return pl.pallas_call(
        share_kernel,
        out_shape=jax.ShapeDtypeStruct((devices, rows, got.shape[2]), got.dtype),
        in_specs=[pl.BlockSpec(memory_space=pltpu.VMEM)],
        name="share_total",
    )(got)


def settle_kernel(asked_ref, got_ref, table_ref, new_ref, rows_ref):
    owners, both = asked_ref.shape
    capacity = both // 2
    embed = got_ref.shape[2]
    table_rows = table_ref.shape[0]
    for p in range(3):
        rows_ref[p, :table_rows] = table_ref[:, p * embed : (p + 1) * embed]

    def place(i, carry):
        for k in range(capacity):
            slot = asked_ref[i, capacity + k]
            for p in range(3):
                at = p * capacity + k
                rows_ref[p, pl.ds(slot, 1), :] = got_ref[i, at : at + 1, :]
        return carry

    lax.fori_loop(0, owners, place, 0)
    for p in range(3):
        new_ref[:, p * embed : (p + 1) * embed] = rows_ref[p, :table_rows]


def settle(asked, got, table):
    table_rows, width = table.shape
    return pl.pallas_call(
        settle_kernel,
        out_shape=jax.ShapeDtypeStruct(table.shape, table.dtype),
        in_specs=[
            pl.BlockSpec(memory_space=pltpu.SMEM),
            pl.BlockSpec(memory_space=pltpu.VMEM),
            pl.BlockSpec(table.shape),
        ],
        out_specs=pl.BlockSpec(table.shape),
        scratch_shapes=[pltpu.VMEM((3, table_rows + 8, width // 3), table.dtype)],
        name="settle",
    )(asked, got, table)


def mask_kernel(counts_ref, got_ref, fetched_ref):
    owners, capacity, width = fetched_ref.shape
    embed = width // 3
    for i in range(owners):
        live = lax.broadcasted_iota(jnp.int32, (capacity, embed), 0) < counts_ref[0, i]
        for p in range(3):
            block = got_ref[i, p * capacity : (p + 1) * capacity, :]
            fetched_ref[i, :, p * embed : (p + 1) * embed] = jnp.where(live, block, 0.0)


def mask_rows(counts, got, capacity):
    return pl.pallas_call(
        mask_kernel,
        out_shape=jax.ShapeDtypeStruct((got.shape[0], capacity, 3 * got.shape[2]), got.dtype),
        in_specs=[pl.BlockSpec(memory_space=pltpu.SMEM), pl.BlockSpec(memory_space=pltpu.VMEM)],
        name="mask_rows",
    )(counts, got)


def finish_kernel(every_ref, out_ref, *, scale):
    _, both, columns = every_ref.shape
    rows = both // 2
    for x in range(side):
        for c in range(2):
            left = (c * side + x) * columns
            for k in range(2):
                for y in range(0, side, 2):
                    pair = [every_ref[(x * side + y + i) * 2 + c, k * rows : (k + 1) * rows] for i in range(2)]
                    top = (k * side + y) * rows
                    out_ref[top : top + both, left : left + columns] = (
                        jnp.concatenate(pair, 0) * scale
                    ).astype(out_ref.dtype)


def finish(every, scale):
    _, rows, columns = every.shape
    return pl.pallas_call(
        functools.partial(finish_kernel, scale=scale),
        out_shape=jax.ShapeDtypeStruct((side * rows, 2 * side * columns), jnp.bfloat16),
        in_specs=[pl.BlockSpec(memory_space=pltpu.VMEM)],
        name="finish",
    )(every)


def pairs(core, x, y):
    bits = (x * side + y) * 2 + core
    return [(d, d ^ bits) for d in range(2 * side * side)]


def send_to(a, x, y):
    return lax.ppermute(a, "dp", pairs(0, x, y))


def on_chip(a):
    return pltpu.with_memory_space_constraint(a, pltpu.VMEM)


def local(
    cache_state,
    table_state,
    batch_idx,
    loss_grad,
    w_first,
    head,
    home,
    fetch_rows,
    fetch_counts,
    evict_rows,
    evict_from,
    evict_counts,
):
    group = lax.axis_size("shard")
    devices = lax.axis_size("dp")
    place = lax.axis_index("dp").astype(jnp.uint32)
    core = (place & 1).astype(jnp.int32)
    cache = cache_state[0, 0]
    table = table_state[0, 0]
    batch_t = batch_idx[0, 0].T
    loss = loss_grad[0]
    wanted = fetch_rows[0, 0]
    gone = evict_rows[0, 0]
    table_rows = table.shape[0]
    capacity = wanted.shape[1]
    samples = loss.shape[1]
    mlp_width = w_first.shape[0]

    info = jnp.stack([1 - core, core, (place >> 3).astype(jnp.int32), ((place >> 1) & 3).astype(jnp.int32)])
    head_row = head[None]
    send, keep, delta_a, delta_b = forward(info, group, cache, batch_t, loss, head_row, w_first)
    partner = lax.ppermute(send, "dp", pairs(1, 0, 0))
    slots = lookup(home, wanted, gone, evict_counts[0], table_rows)
    partner, slots = lax.optimization_barrier((partner, slots))
    even_in = send_to(keep[1] + partner[1], 1, 0)
    odd_in = send_to(keep[3] + partner[3], 0, 1)
    sent = backward(info, evict_from[0, 0], cache, slots, batch_t, on_chip(delta_a), on_chip(delta_b), w_first)
    got = lax.all_to_all(sent, "shard", split_axis=0, concat_axis=0, tiled=True)
    even = keep[0] + partner[0] + even_in
    odd = keep[2] + partner[2] + odd_in
    even = even[0] + send_to(even[1], 0, 1)
    odd = odd[0] + send_to(odd[1], 1, 0)
    mine = jnp.stack([even[0], odd[0]], 1) + send_to(jnp.stack([even[1], odd[1]], 1), 3, 0)
    other = send_to(mine[1], 0, 3)
    asked = got[:, 3 * capacity, : 2 * capacity].astype(jnp.int32)
    served = serve(asked, table, 2 * mine.shape[3])
    served = add_block(on_chip(mine[0]), on_chip(other), served)
    came = on_chip(lax.all_to_all(served, "shard", split_axis=0, concat_axis=0, tiled=True))
    new_table = settle(asked, on_chip(got), table)
    scale = 1.0 / math.sqrt(samples * group * devices)
    every = share_total(came, mlp_width // (group * side), devices)
    every = on_chip(lax.all_to_all(every, "dp", split_axis=0, concat_axis=0, tiled=True))
    fetched = mask_rows(fetch_counts[0], came, capacity)
    grad_first = finish(every, scale)
    return (grad_first, new_table[None, None], fetched[None, None])


def solution(mesh):
    placed = (
        P("dp", "shard", None, None),
        P("dp", "shard", None, None),
        P("dp", "shard", None, None),
        P("dp", "shard", None),
        P(),
        P(),
        P("dp", None),
        P("dp", "shard", None, None),
        P("dp", "shard", None),
        P("dp", "shard", None, None),
        P("dp", "shard", None, None),
        P("dp", "shard", None),
    )

    return jax.shard_map(
        local,
        mesh=mesh,
        in_specs=placed,
        out_specs=(
            P("shard", None),
            P("dp", "shard", None, None),
            P("dp", "shard", None, None, None),
        ),
        check_vma=False,
    )
```
